32 devices in a mesh: groups: 2 (over y), expert: 4 (over z), section: 4 (over x, core).
Axes of the slice: x: 2, y: 2, z: 4, core: 2. Of those that a mesh axis runs over, the one named last changes fastest.
Arguments:
- layer_inputs: bfloat16 [4, 2, 512, 1024], P('section', None, ('groups', 'expert')), parts along dimension 2, may hold values from -6 to 6
- out_cotangent: bfloat16 [2, 512, 1024], P(None, ('groups', 'expert')), parts along dimension 1, may hold values from -0.59765625 to 0.59765625
- expert_routes: int32 [4, 2, 512, 2], P('section', None, 'groups'), parts along dimension 2, may hold values from 0 to 3, all different within a row; in each aligned block of 64 rows (0 to 63, 64 to 127, ..., all dimensions but the last counted through in order) at most 40 rows name the same one
- norm_gain: float32 [4, 1024], P('section'), may hold values from 0.5 to 1.5
- router_weight: float32 [4, 4, 1024], P('section'), may hold values from -0.1875 to 0.1875
- up_weight: bfloat16 [4, 1024, 16384], P('section', None, 'expert'), may hold values from -0.1875 to 0.1875
- down_weight: bfloat16 [4, 16384, 1024], P('section', 'expert'), may hold values from -0.09375 to 0.09375
Outputs:
- up_grad: bfloat16 [4, 2048, 16384], P('section', 'groups', 'expert'), parts along dimension 1
- down_grad: bfloat16 [4, 16384, 2048], P('section', 'expert', 'groups'), parts along dimension 2
- router_grad: float32 [4, 8, 1024], P('section', 'groups'), parts along dimension 1
- gain_grad: float32 [4, 2048], P('section', 'groups'), parts along dimension 1
The draws below stay inside these ranges and needn't reach their ends.
There are 2 independent parts, one for each index of `groups`. The reference program is written for one: setup_inputs(seed, part) draws one part's arguments, and reference() takes and returns one part's arrays. A program takes and returns all parts, laid end to end along the dimension named above; an argument that names none is the same for every part. Nothing has to cross between parts.
Inputs may be any that keep to these rules, and one draw needn't show every extreme that they name: `expert_routes`: in every aligned block of 64 tokens (the tokens of one index of expert, for one sublayer and micro-batch), each expert is listed by at most 40 tokens; the two experts of a token differ.
All inputs are finite; a program needn't handle non-finite values.
Results may differ from the reference program's by a relative error of at most 0.025.
Values may be sent and summed in bfloat16 or wider, within the bound.
No kernel may reach another device: no remote copies, remote signals or barrier semaphores. Data moves between devices by JAX's collectives and lax.ppermute only.
A program may use at most 192 MiB of HBM per device.

```python
import math
import jax
import jax.numpy as jnp
import numpy as np
from jax import lax

D = 1024
FF = 4096
EXPERTS = 4
TOP = 2
MICRO = 2
ROWS = 64
CAP = 40
LAYERS = 4
TOKENS = 256
N_EXPERT = 4


def shard_levels(stream_key, dims, split, least, high):
    loudness, own = 1.0, jax.random.fold_in(stream_key, 6)
    for axis_at, parts in split:
        steps = jnp.exp(jax.random.uniform(jax.random.fold_in(own, axis_at), (parts,), jnp.float32, least / len(split), high / len(split)))
        loudness = loudness * jnp.repeat(steps, dims[axis_at] // parts).reshape([-1 if axis == axis_at else 1 for axis in range(len(dims))])
    return loudness


def routed_block(stream_key, own, number, rows, number_of, top, bound, skew):
    order = jax.random.permutation(stream_key, number_of)
    packed, usual = portions_of(number_of, rows * top, bound, skew, True), portions_of(number_of, rows * top, bound, skew, False)
    places = jnp.arange(number_of)

    def named(sizes, rotation):
        used = int((sizes > 0).sum())
        fixed = max(1, used // 4)
        passed = fixed + (places - fixed + rotation * (used - fixed)) % max(1, number_of - fixed)
        return jnp.zeros((number_of,), jnp.int32).at[order[jnp.where(places < fixed, places, passed)]].set(jnp.asarray(sizes, jnp.int32))

    sizes = jnp.where(number % 4 == 0, named(packed, number // 4), named(usual, number - number // 4 - 1))
    mixed = jax.random.permutation(jax.random.fold_in(own, 3), number_of)
    donor, sink = mixed[0:number_of // 2 * 2:2], mixed[1:number_of // 2 * 2:2]
    margin = jnp.minimum(sizes[donor] - 1, bound - sizes[sink]) // 2
    margin = jnp.where((donor == order[0]) | (sink == order[0]) | (sizes[sink] == 0), 0, jnp.maximum(margin, 0))
    passed = jax.random.randint(jax.random.fold_in(own, 4), (number_of // 2,), 0, 1 << 20) % (margin + 1)
    sizes = sizes.at[donor].add(-passed).at[sink].add(passed)
    items = jnp.searchsorted(jnp.cumsum(sizes), jnp.arange(rows * top), side="right").astype(jnp.int32)
    table = items.reshape(top, rows).T
    table = table[jax.random.permutation(jax.random.fold_in(own, 1), rows)]
    rotation = jax.random.randint(jax.random.fold_in(own, 2), (rows, 1), 0, top)
    return jnp.take_along_axis(table, (jnp.arange(top)[None, :] + rotation) % top, axis=1)


def portions_of(number_of, total, limit, slope, full):
    weights = [(1 << 20) // math.isqrt(rank ** slope) + 1 for rank in range(1, number_of + 1)]
    largest = limit if full else min(limit, max(-(-total // number_of), total * weights[0] // sum(weights)))
    least = 1 if total - largest >= number_of - 1 else 0
    holding, spare = [largest] + [least] * (number_of - 1), total - largest - least * (number_of - 1)
    while spare > 0:
        free = [i for i in range(1, number_of) if holding[i] < largest] or [i for i in range(1, number_of) if holding[i] < limit]
        pool, remaining = sum([weights[i] for i in free]), spare
        for i in free:
            extra = min(limit - holding[i], max(1, remaining * weights[i] // pool), spare)
            holding[i] = holding[i] + extra
            spare = spare - extra
    return np.array(holding)


def normal_values(rng, dims, width, reach, split=(), kind=jnp.bfloat16):
    factor_of = shard_levels(rng, dims, split, -0.22, 0.18) if split else 1.0
    values = jax.random.normal(rng, dims, jnp.float32) * width * factor_of
    return jnp.minimum(jnp.maximum(values, -reach), reach).astype(kind)


def setup_inputs(seed: int = 0, part: int = 0) -> dict:
    key_of = jax.random.split(jax.random.key(seed), 8)
    own_keys = jax.random.split(jax.random.fold_in(key_of[7], part), 8)
    layer_inputs = normal_values(own_keys[0], (LAYERS, MICRO, TOKENS, D), 1.0, 6.0, ((0, 4), (2, 4)))
    out_cotangent = normal_values(own_keys[1], (MICRO, TOKENS, D), 0.1, 0.59765625, ((1, 4),))
    expert_routes_keys = jax.random.split(jax.random.fold_in(own_keys[2], 1), LAYERS * MICRO * TOKENS // ROWS)
    expert_routes_turns = jax.random.permutation(jax.random.fold_in(own_keys[2], 3), LAYERS * MICRO * TOKENS // ROWS)
    expert_routes = jax.vmap(lambda own, number: routed_block(jax.random.fold_in(own_keys[2], 2), own, number, ROWS, EXPERTS, TOP, CAP, 2))(expert_routes_keys, expert_routes_turns).reshape((LAYERS, MICRO, TOKENS, TOP))
    norm_gain = jnp.clip(1.0 + 0.1 * jax.random.normal(key_of[3], (LAYERS, D), jnp.float32), 0.5, 1.5)
    router_weight = normal_values(key_of[4], (LAYERS, EXPERTS, D), D ** -0.5, 0.1875, ((0, 4),), jnp.float32)
    up_weight = normal_values(key_of[5], (LAYERS, D, EXPERTS * FF), D ** -0.5, 0.1875, ((0, 4), (2, 4)))
    down_weight = normal_values(key_of[6], (LAYERS, EXPERTS * FF, D), FF ** -0.5, 0.09375, ((0, 4), (1, 4)))
    return dict(layer_inputs=layer_inputs, out_cotangent=out_cotangent, expert_routes=expert_routes, norm_gain=norm_gain, router_weight=router_weight, up_weight=up_weight, down_weight=down_weight)


norm_eps = 1e-06
gelu_coef = 0.7978845608028654
cubic_coef = 0.044715
highest = lax.Precision.HIGHEST

def gelu_parts(pre_act):
    inner_arg = gelu_coef * (pre_act + cubic_coef * pre_act * pre_act * pre_act)
    tanh_val = jnp.tanh(inner_arg)
    values = 0.5 * pre_act * (1.0 + tanh_val)
    slopes = 0.5 * (1.0 + tanh_val) + 0.5 * pre_act * (1.0 - tanh_val * tanh_val) * gelu_coef * (1.0 + 3.0 * cubic_coef * pre_act * pre_act)
    return (values, slopes)

def norm_rows(row_vals, gain_vec):
    values = row_vals.astype(jnp.float32)
    mean_sq = lax.optimization_barrier(jnp.mean(values * values, axis=-1, keepdims=True))
    inverse = lax.rsqrt(mean_sq + norm_eps)
    normed = values * inverse
    return ((normed * gain_vec).astype(jnp.bfloat16), normed, inverse)

def route_weights(normed_low, router, chosen):
    logits = jnp.einsum('...d,ed->...e', normed_low.astype(jnp.float32), router, precision=highest)
    scores = jax.nn.sigmoid(logits)
    expert_ids = lax.broadcasted_iota(jnp.int32, scores.shape, scores.ndim - 1)
    first_hot = (chosen[..., 0:1] == expert_ids).astype(jnp.float32)
    second_hot = (chosen[..., 1:2] == expert_ids).astype(jnp.float32)
    totals = lax.optimization_barrier(jnp.sum(scores * (first_hot + second_hot), axis=-1, keepdims=True))
    weights = scores * (first_hot + second_hot) / totals
    return (scores, first_hot, second_hot, totals, weights)

def owner_back(grad_in, expert_grad, combine_grad, route_parts, normed_low, normed, inverse, gain_vec, router):
    scores, first_hot, second_hot, totals, weights = route_parts
    first_grad = lax.optimization_barrier(jnp.sum(combine_grad * first_hot, axis=-1, keepdims=True))
    second_grad = lax.optimization_barrier(jnp.sum(combine_grad * second_hot, axis=-1, keepdims=True))
    first_wt = lax.optimization_barrier(jnp.sum(weights * first_hot, axis=-1, keepdims=True))
    second_wt = lax.optimization_barrier(jnp.sum(weights * second_hot, axis=-1, keepdims=True))
    mean_grad = first_wt * first_grad + second_wt * second_grad
    sig_slope = scores * (1.0 - scores)
    logit_grad = (first_hot * (first_grad - mean_grad) + second_hot * (second_grad - mean_grad)) / totals * sig_slope
    full_grad = expert_grad + jnp.dot(logit_grad, router, precision=highest)
    scaled_grad = full_grad * gain_vec
    center = lax.optimization_barrier(jnp.mean(scaled_grad * normed, axis=-1, keepdims=True))
    input_grad = (grad_in.astype(jnp.float32) + inverse * (scaled_grad - normed * center)).astype(jnp.bfloat16)
    router_term = jnp.dot(logit_grad.T, normed_low.astype(jnp.float32), precision=highest)
    gain_term = lax.optimization_barrier(jnp.sum(full_grad * normed, axis=0))
    return (input_grad, router_term, gain_term)

def layer_back(inputs, grad_in, chosen, gain_vec, router, up_full, down_full):
    normed_low, normed, inverse = norm_rows(inputs, gain_vec)
    route_parts = route_weights(normed_low, router, chosen)
    weights = route_parts[4]
    hit_mask = route_parts[1] + route_parts[2]
    tokens, feat_dim = inputs.shape
    experts = router.shape[0]
    hidden = up_full.shape[1] // experts
    slices = N_EXPERT // experts
    block_len = hidden // slices
    grad_f32 = grad_in.astype(jnp.float32)
    expert_grad = jnp.zeros((tokens, feat_dim), jnp.float32)
    combine_grad = jnp.zeros((tokens, experts), jnp.float32)
    expert_ids = lax.broadcasted_iota(jnp.int32, (1, experts), 1)
    up_terms = []
    down_terms = []
    for expert in range(experts):
        up_cols = up_full[:, expert * hidden:(expert + 1) * hidden]
        down_rows = down_full[expert * hidden:(expert + 1) * hidden, :]
        expert_wt = weights[:, expert:expert + 1]
        expert_hit = hit_mask[:, expert:expert + 1]
        pre_act = jnp.dot(normed_low, up_cols, preferred_element_type=jnp.float32)
        act_vals, slopes = gelu_parts(pre_act)
        act_low = act_vals.astype(jnp.bfloat16)
        back_hidden = jnp.dot(grad_in, down_rows.T, preferred_element_type=jnp.float32)
        block_sums = lax.optimization_barrier(jnp.sum((act_low.astype(jnp.float32) * back_hidden).reshape(tokens, slices, block_len), axis=-1))
        block_sums = lax.optimization_barrier(block_sums.astype(jnp.bfloat16)).astype(jnp.float32)
        combine_col = lax.optimization_barrier(jnp.sum(block_sums, axis=-1, keepdims=True)) * expert_hit
        combine_grad = combine_grad + combine_col * (expert_ids == expert).astype(jnp.float32)
        hidden_grad = (expert_wt * back_hidden * slopes).astype(jnp.bfloat16)
        pieces = jnp.einsum('tsk,dsk->std', hidden_grad.astype(jnp.float32).reshape(tokens, slices, block_len), up_cols.astype(jnp.float32).reshape(feat_dim, slices, block_len))
        pieces = lax.optimization_barrier(pieces.astype(jnp.bfloat16)).astype(jnp.float32)
        expert_grad = expert_grad + lax.optimization_barrier(jnp.sum(pieces, axis=0))
        scaled = (expert_wt * grad_f32).astype(jnp.bfloat16)
        up_terms.append(jnp.dot(normed_low.T, hidden_grad, preferred_element_type=jnp.float32))
        down_terms.append(jnp.dot(act_low.T, scaled, preferred_element_type=jnp.float32))
    input_grad, router_term, gain_term = owner_back(grad_in, expert_grad, combine_grad, route_parts, normed_low, normed, inverse, gain_vec, router)
    return (input_grad, jnp.concatenate(up_terms, axis=1), jnp.concatenate(down_terms, axis=0), router_term, gain_term)

def reference(layer_inputs, out_cotangent, expert_routes, norm_gain, router_weight, up_weight, down_weight):
    layers = layer_inputs.shape[0]
    micro_count = layer_inputs.shape[1]
    grad_list = [out_cotangent[micro_no] for micro_no in range(micro_count)]
    up_out = [None] * layers
    down_out = [None] * layers
    router_out = [None] * layers
    gain_out = [None] * layers
    for layer_no in range(layers - 1, -1, -1):
        up_sum = jnp.zeros(up_weight.shape[1:], jnp.float32)
        down_sum = jnp.zeros(down_weight.shape[1:], jnp.float32)
        router_sum = jnp.zeros(router_weight.shape[1:], jnp.float32)
        gain_sum = jnp.zeros(norm_gain.shape[1:], jnp.float32)
        for micro_no in range(micro_count):
            result = layer_back(layer_inputs[layer_no, micro_no], grad_list[micro_no], expert_routes[layer_no, micro_no], norm_gain[layer_no], router_weight[layer_no], up_weight[layer_no], down_weight[layer_no])
            grad_list[micro_no] = result[0]
            up_sum = up_sum + result[1]
            down_sum = down_sum + result[2]
            router_sum = router_sum + result[3]
            gain_sum = gain_sum + result[4]
        up_out[layer_no] = up_sum
        down_out[layer_no] = down_sum
        router_out[layer_no] = router_sum
        gain_out[layer_no] = gain_sum
    return (jnp.stack(up_out).astype(jnp.bfloat16), jnp.stack(down_out).astype(jnp.bfloat16), jnp.stack(router_out), jnp.stack(gain_out))
```

```python
import functools

import jax
import jax.numpy as jnp
from jax import lax
from jax.experimental import pallas as pl
from jax.experimental.pallas import tpu as pltpu
from jax.sharding import PartitionSpec as P

norm_eps = 1e-06
gelu_coef = 0.7978845608028654
cubic_coef = 0.044715
BLOCK_ROWS = 64
BLOCK_CAP = 40
F32 = jnp.float32
BF16 = jnp.bfloat16
AUX = 8


def vmem():
    return pl.BlockSpec(memory_space=pltpu.VMEM)


def smem():
    return pl.BlockSpec(memory_space=pltpu.SMEM)


def params(mebi=24):
    return pltpu.CompilerParams(vmem_limit_bytes=mebi * 1024 * 1024)


def cost(flops, nbytes):
    return pl.CostEstimate(flops=int(flops), bytes_accessed=int(nbytes), transcendentals=0)


def dot(a, b, dims):
    return lax.dot_general(a, b, ((dims[0:1], dims[1:2]), ((), ())), preferred_element_type=F32)


def iota(shape, dim):
    return lax.broadcasted_iota(jnp.int32, shape, dim)


def row_norm(values):
    mean_sq = jnp.mean(values * values, axis=-1, keepdims=True)
    return lax.rsqrt(mean_sq + norm_eps)


def eye(size):
    return (iota((size, size), 0) == iota((size, size), 1)).astype(F32)


def prep_kernel(
    shards, slices, rows, slots, cap, place, x_far, cot_far, up_far, col_ref, row_ref, gain_ref, router_ref, *outs
):
    x_ref, cot_ref, sems = outs[-3:]
    up_ref = outs[-4]
    outs = outs[:-4]
    loads = [
        pltpu.make_async_copy(source, target, sems.at[index])
        for index, (source, target) in enumerate([(x_far, x_ref), (cot_far, cot_ref), (up_far, up_ref)])
    ]
    for load in loads:
        load.start()
    loads[0].wait()
    loads[1].wait()
    h_outs, c_outs = outs[:shards], outs[shards : 2 * shards - 1]
    gather_ref, scatter_ref, score_ref, own_ref = outs[2 * shards - 1 :]
    me = place[0]
    is_last = place[1] == place[2]
    total = x_ref.shape[0]
    experts = router_ref.shape[0]
    x = x_ref[...].astype(F32)
    h32 = (x * row_norm(x)) * gain_ref[...]
    h = h32.astype(BF16)
    logits = lax.dot_general(
        h.astype(F32), router_ref[...], (((1,), (1,)), ((), ())),
        preferred_element_type=F32, precision=lax.Precision.HIGHEST,
    )
    scores = 1.0 / (1.0 + jnp.exp(-logits))
    ids = iota((total, experts), 1)
    hits = jnp.logical_or(col_ref[:, 0:1] == ids, col_ref[:, 1:2] == ids).astype(F32)
    totals = jnp.sum(scores * hits, axis=-1, keepdims=True)
    weights = scores * hits / totals
    score_ref[0] = scores
    score_ref[1] = weights
    score_ref[2] = hits
    score_ref[3] = jnp.broadcast_to(totals, (total, experts))
    first, second = iota((total, total), 0), iota((total, total), 1)
    same = (first // rows) == (second // rows)
    before = jnp.logical_and(same, second < first).astype(BF16)
    after = jnp.logical_and(same, first < second).astype(BF16)
    base_col = (iota((total, experts), 0) // rows * cap).astype(F32)
    slot_col = jnp.where(hits > 0.0, dot(before, hits.astype(BF16), (1, 0)) + base_col, -1.0)
    ids_row = iota((experts, total), 0)
    hits_row = jnp.logical_or(row_ref[0:1, :] == ids_row, row_ref[1:2, :] == ids_row).astype(F32)
    base_row = (iota((experts, total), 1) // rows * cap).astype(F32)
    slot_row = jnp.where(hits_row > 0.0, dot(hits_row.astype(BF16), after, (1, 0)) + base_row, -1.0)
    cot = cot_ref[...]
    own_ref[...] = jnp.where(is_last, cot.astype(F32), 0.0).astype(BF16)
    slot_lane = iota((total, slots), 1).astype(F32)
    slot_sub = iota((slots, total), 0).astype(F32)
    for step in range(shards):
        expert = lax.rem(me + step, shards) // slices
        mine = (ids == expert).astype(F32)
        slot_c = jnp.sum(slot_col * mine, axis=-1, keepdims=True)
        slot_r = jnp.sum(slot_row * (ids_row == expert).astype(F32), axis=0, keepdims=True)
        scatter = (slot_c == slot_lane).astype(F32)
        gather = (slot_r == slot_sub).astype(F32).astype(BF16)
        weight_c = jnp.sum(weights * mine, axis=-1, keepdims=True)
        weight_r = jnp.sum(scatter * weight_c, axis=0, keepdims=True)
        high = weight_r.astype(BF16).astype(F32)
        low = weight_r - high
        aux_id = iota((AUX, slots), 0)
        aux = jnp.where(aux_id == 0, high, jnp.where(aux_id == 1, low, 0.0)).astype(BF16)
        picked = dot(gather, h, (1, 0)).astype(BF16)
        for target in [h_outs[step]] + ([c_outs[step - 1]] if step else []):
            target[0:slots, :] = picked
            target[slots : slots + AUX, :] = jnp.zeros((AUX, x.shape[1]), BF16)
            target[slots : slots + AUX, 0:slots] = aux
        if step:
            c_outs[step - 1][slots + AUX :, :] = dot(gather, cot, (1, 0)).astype(BF16)
        gather_ref[step] = gather
        scatter_ref[step] = scatter.astype(BF16)
    loads[2].wait()


def forward_kernel(slots, width, loads, own, others, *refs):
    refs = list(refs)[1:]
    take = lambda n: [refs.pop(0) for _ in range(n)]
    if loads:
        sem = refs.pop()
        load = pltpu.make_async_copy(take(1)[0], refs.pop(), sem)
        load.start()
    sources = [take(1) for _ in range(own)] + [take(2) for _ in range(others)]
    up_ref = take(1)[0]
    act_ref, slope_ref, rows_ref, wt_ref = refs[-4:]
    for index, source in enumerate(sources):
        span = slice(index * slots, (index + 1) * slots)
        value = source[0][0 : slots + AUX, :].astype(F32)
        for extra in source[1:]:
            value = value + extra[0 : slots + AUX, :].astype(F32)
        rows_ref[span, :] = value[0:slots, :].astype(BF16)
        weight_r = value[slots : slots + 1, 0:slots] + value[slots + 1 : slots + 2, 0:slots]
        wt_ref[span, :] = jnp.sum(eye(slots) * weight_r, axis=-1, keepdims=True)

    def block(index, carry):
        span = pl.ds(pl.multiple_of(index * width, width), width)
        u = dot(rows_ref[...], up_ref[:, span], (1, 0))
        square = u * u
        tanh_val = jnp.tanh(gelu_coef * (u + cubic_coef * square * u))
        half = 0.5 * (1.0 + tanh_val)
        act_ref[:, span] = (u * half).astype(BF16)
        slope = half + 0.5 * u * (1.0 - tanh_val * tanh_val) * (gelu_coef * (1.0 + 3.0 * cubic_coef * square))
        slope_ref[:, span] = (slope * wt_ref[...]).astype(BF16)
        return carry

    lax.fori_loop(0, up_ref.shape[1] // width, block, 0)
    if loads:
        load.wait()


def back_kernel(slots, width, base, stage, keep, has_after, has_own, has_prev, others, place, *refs):
    refs = list(refs)[1:] if has_after else list(refs)
    reached = place[1] + stage >= place[2]
    take = lambda n: [refs.pop(0) for _ in range(n)]
    own_count = (2 if has_prev else 1) if has_own else 0
    own_in = take(own_count)
    gather_ref = take(1)[0] if has_own else None
    recv_in = take(others)
    prev_in = take(others) if has_prev else None
    up_ref, down_ref, act_ref, slope_ref = take(4)
    own_out = take(1)[0] if has_own else None
    cot_ref = take(1)[0]
    q_ref = take(1)[0] if keep else None
    parts = take(others + (1 if has_own else 0))
    acc_ref = take(1)[0]
    shift = 1 if has_own else 0
    if has_own:
        own = own_in[0][...]
        if has_prev:
            own = (own.astype(F32) + own_in[1][...].astype(F32)).astype(BF16)
        own_out[...] = own
        cot_ref[0:slots, :] = dot(gather_ref[0], own, (1, 0)).astype(BF16)
    for place in range(others):
        value = recv_in[place][base : base + slots, :]
        if has_prev:
            old = prev_in[place][(place + shift) * slots : (place + shift + 1) * slots, :]
            value = (value.astype(F32) + old.astype(F32)).astype(BF16)
        cot_ref[(place + shift) * slots : (place + shift + 1) * slots, :] = value

    @pl.when(reached)
    def _():
        hidden = down_ref.shape[0]
        lanes = 128
        acc_ref[...] = jnp.zeros_like(acc_ref)

        def block(index, comb):
            span = pl.ds(pl.multiple_of(index * width, width), width)
            t = dot(cot_ref[...], down_ref[span, :], (1, 1))
            prod = act_ref[:, span].astype(F32) * t
            for start in range(0, width, lanes):
                comb = comb + prod[:, start : start + lanes]
            q = (slope_ref[:, span].astype(F32) * t).astype(BF16)
            if keep:
                q_ref[:, span] = q
            acc_ref[...] += dot(q, up_ref[:, span], (1, 1))
            return comb

        comb = lax.fori_loop(0, hidden // width, block, jnp.zeros((cot_ref.shape[0], lanes), F32))
        for place, part in enumerate(parts):
            span = slice(place * slots, (place + 1) * slots)
            part[0:slots, :] = acc_ref[span, :].astype(BF16)
            comb_c = jnp.sum(comb[span, :], axis=-1, keepdims=True)
            comb_r = jnp.sum(eye(slots) * comb_c, axis=0, keepdims=True)
            part[slots : slots + AUX, :] = jnp.zeros((AUX, part.shape[1]), BF16)
            part[slots : slots + AUX, 0:slots] = jnp.broadcast_to(comb_r, (AUX, slots)).astype(BF16)


def owner_kernel(shards, slices, slots, stage, want_next, place, *refs):
    refs = list(refs) if want_next else list(refs)[1:]
    parts = refs[:shards]
    own_ref, x_ref, gain_ref, router_ref, score_ref, scatter_ref, acc_ref = refs[shards : shards + 7]
    refs = refs[shards + 7 :]
    me = place[0]
    active = place[1] == place[2] - stage
    if want_next:
        gather_ref, acc_out, own_out = refs[0:3]
        sends = refs[3:]
    else:
        (acc_out,) = refs

    @pl.when(jnp.logical_not(active))
    def _():
        acc_out[...] = acc_ref[...]

    @pl.when(active)
    def _():
        experts = router_ref.shape[0]
        total = x_ref.shape[0]
        ids = iota((total, experts), 1)
        gh = jnp.zeros(x_ref.shape, F32)
        comb = jnp.zeros((total, experts), F32)
        for step in range(shards):
            expert = lax.rem(me + step, shards) // slices
            scatter = scatter_ref[step]
            gh = gh + dot(scatter, parts[step][0:slots, :], (1, 0))
            comb_r = parts[step][slots : slots + AUX, 0:slots].astype(F32)[0:1, :]
            comb_c = jnp.sum(scatter.astype(F32) * comb_r, axis=-1, keepdims=True)
            comb = comb + comb_c * (ids == expert).astype(F32)
        scores, weights, hits, totals = (score_ref[i] for i in range(4))
        center_comb = jnp.sum(weights * comb, axis=-1, keepdims=True)
        logit_grad = hits * (comb - center_comb) / totals * (scores * (1.0 - scores))
        for expert in range(experts):
            gh = gh + logit_grad[:, expert : expert + 1] * router_ref[expert : expert + 1, :]
        x = x_ref[...].astype(F32)
        inverse = row_norm(x)
        normed = x * inverse
        gain = gain_ref[...]
        if want_next:
            scaled = gh * gain
            center = jnp.mean(scaled * normed, axis=-1, keepdims=True)
            gx = (own_ref[...].astype(F32) + inverse * (scaled - normed * center)).astype(BF16)
            own_out[...] = gx
            for step in range(1, shards):
                sends[step - 1][...] = dot(gather_ref[step], gx, (1, 0)).astype(BF16)
        h = (normed * gain).astype(BF16).astype(F32)
        terms = [
            jnp.sum(logit_grad[:, expert : expert + 1] * h, axis=0, keepdims=True) for expert in range(experts)
        ]
        terms.append(jnp.sum(gh * normed, axis=0, keepdims=True))
        for index, term in enumerate(terms):
            acc_out[index : index + 1, :] = term
        rest = acc_out.shape[0] - len(terms)
        if rest:
            acc_out[len(terms) :, :] = jnp.zeros((rest, x.shape[1]), F32)


def up_kernel(count, *refs):
    rows, qs = refs[:count], refs[count : 2 * count]
    out_ref, mark_ref = refs[2 * count : 2 * count + 2]
    turned = refs[2 * count + 2 :]

    @pl.when(pl.program_id(0) == 0)
    def _():
        mark_ref[...] = jnp.zeros_like(mark_ref)
        for index in range(count):
            turned[index][...] = rows[index][...].astype(F32).T.astype(BF16)

    total = dot(turned[0][...], qs[0][...], (1, 0))
    for index in range(1, count):
        total = total + dot(turned[index][...], qs[index][...], (1, 0))
    out_ref[...] = total.astype(BF16)


def down_kernel(count, after, *refs):
    cots, wts, acts = (refs[i * count : (i + 1) * count] for i in range(3))
    out_ref = refs[3 * count]
    y_refs = refs[3 * count + 1 :]

    @pl.when(pl.program_id(0) == 0)
    def _():
        for index in range(count):
            y_refs[index][...] = (wts[index][...] * cots[index][...].astype(F32)).astype(BF16)

    total = dot(acts[0][...], y_refs[0][...], (0, 0))
    for index in range(1, count):
        total = total + dot(acts[index][...], y_refs[index][...], (0, 0))
    out_ref[...] = total.astype(BF16)


def finish_kernel(shards, experts, *refs):
    total = refs[0][...]
    for ref in refs[1:shards]:
        total = total + ref[...]
    refs[shards][...] = total[0:experts, :]
    refs[shards + 1][...] = total[experts : experts + 1, :]


def body(
    layer_inputs, out_cotangent, expert_routes, norm_gain, router_weight, up_weight, down_weight
):
    sections = lax.axis_size("section")
    section_id = lax.axis_index("section")
    shards = lax.axis_size("expert")
    shard_id = lax.axis_index("expert")
    micro, rows, feat = layer_inputs.shape[1:]
    router = router_weight[0]
    experts = router.shape[0]
    up = up_weight[0]
    down = down_weight[0]
    hidden = up.shape[1]
    slices = shards // experts
    total = micro * rows
    cap = rows // BLOCK_ROWS * BLOCK_CAP if rows % BLOCK_ROWS == 0 else rows
    slots = micro * cap
    sent = slots + AUX
    last = sections - 1
    x = layer_inputs[0].reshape(total, feat)
    cot = out_cotangent.reshape(total, feat)
    chosen = lax.dynamic_slice_in_dim(expert_routes[0], shard_id * rows, rows, 1).reshape(total, 2)
    gain = norm_gain
    place = jnp.stack([shard_id, section_id, jnp.int32(last)]).astype(jnp.int32)
    steps = list(range(shards))
    split = max(1, shards // 2)
    chunks = [steps[:split], steps[split:]]
    chunks = [chunk for chunk in chunks if chunk]
    width = min(1024, hidden)
    blocks = hidden // width

    def sds(shape, dtype=BF16):
        return jax.ShapeDtypeStruct(shape, dtype)

    def move(value, pairs):
        flat = [(sz * sections + ss, dz * sections + ds) for (ss, sz), (ds, dz) in pairs]
        return lax.ppermute(value, ("expert", "section"), flat)

    def spread(value, step, sources, drop):
        return move(
            value,
            [((s, z), (s - drop, (z + step) % shards)) for s in sources for z in range(shards) if s - drop >= 0],
        )

    def any_place():
        return pl.BlockSpec(memory_space=pl.ANY)

    everyone = list(range(sections))
    far = [pltpu.with_memory_space_constraint(array, pltpu.HBM) for array in (x, cot, up)]
    prep = pl.pallas_call(
        functools.partial(prep_kernel, shards, slices, rows, slots, cap),
        out_shape=[sds((sent, feat))] * shards
        + [sds((sent + slots, feat))] * (shards - 1)
        + [sds((shards, slots, total)), sds((shards, total, slots)), sds((4, total, experts), F32), sds((total, feat))]
        + [pltpu.VMEM(up.shape, BF16)],
        in_specs=[smem()] + [pl.BlockSpec(memory_space=pltpu.HBM)] * 3 + [vmem()] * 4,
        out_specs=[vmem()] * (2 * shards + 4),
        scratch_shapes=[pltpu.VMEM((total, feat), BF16)] * 2 + [pltpu.SemaphoreType.DMA((3,))],
        compiler_params=params(),
        cost_estimate=cost(1e7, 4e6),
        name="prep",
    )(place, *far, chosen, chosen.T, gain, router)
    up_near = prep[-1]
    h_send, c_send = prep[:shards], [None] + list(prep[shards : 2 * shards - 1])
    gather, scatter, score, own = prep[2 * shards - 1 : -1]
    first_recv = [None] + [spread(c_send[step], step, [last], 0) for step in steps[1:]]
    h_recv = [None] + [spread(h_send[step], step, everyone[:-1], 0) for step in steps[1:]]
    gather_next = move(gather, [((s - 1, z), (s, z)) for s in everyone[1:] for z in range(shards)])
    down_far = pltpu.with_memory_space_constraint(down, pltpu.HBM)

    def const(block):
        return pl.BlockSpec(block, lambda i: (0,) * len(block))

    def chunk_rows(chunk):
        return len(chunk) * slots

    def col_block(chunk):
        return pl.BlockSpec((chunk_rows(chunk), width), lambda i: (0, i))

    def forward(chunk, after, load):
        count = chunk_rows(chunk)
        own_part = 1 if chunk[0] == 0 else 0
        args, specs = [after], [any_place()]
        if load is not None:
            args.append(load)
            specs.append(pl.BlockSpec(memory_space=pltpu.HBM))
        args += [h_send[0]] * own_part
        for step in chunk[own_part:]:
            args += [first_recv[step], h_recv[step]]
        args += [pltpu.with_memory_space_constraint(up_near, pltpu.VMEM)]
        specs += [vmem()] * (len(args) - len(specs))
        return list(pl.pallas_call(
            functools.partial(forward_kernel, slots, width, load is not None, own_part, len(chunk) - own_part),
            out_shape=[sds((count, hidden))] * 2
            + [sds((count, feat)), sds((count, 1), F32)]
            + ([pltpu.VMEM(load.shape, BF16)] if load is not None else []),
            in_specs=specs,
            out_specs=[vmem()] * (4 if load is None else 5),
            scratch_shapes=[] if load is None else [pltpu.SemaphoreType.DMA(())],
            compiler_params=params(),
            cost_estimate=cost(2 * count * feat * hidden, 2 * feat * hidden),
            name="forward",
        )(*args))

    def back(stage, chunk, act, slope, recv, base, own_recv, own, prev, after):
        has_own = chunk[0] == 0
        has_prev = prev is not None
        keep = stage == last
        others = [step for step in chunk if step]
        args, specs = [place], [smem()]
        if after is not None:
            args.append(after)
            specs.append(any_place())
        if has_own:
            args += ([own_recv, own] if has_prev else [own]) + [gather]
        args += [recv[step] for step in others]
        if has_prev:
            args += [prev] * len(others)
        args += [pltpu.with_memory_space_constraint(array, pltpu.VMEM) for array in (up_near, down_near)]
        args += [act, slope]
        specs += [vmem()] * (len(args) - len(specs))
        count = chunk_rows(chunk)
        outs = pl.pallas_call(
            functools.partial(back_kernel, slots, width, base, stage, keep, after is not None, has_own, has_prev, len(others)),
            out_shape=([sds((total, feat))] if has_own else [])
            + [sds((count, feat))]
            + ([sds((count, hidden))] if keep else [])
            + [sds((sent, feat))] * len(chunk),
            in_specs=specs,
            out_specs=[vmem()] * (int(has_own) + 1 + int(keep) + len(chunk)),
            scratch_shapes=[pltpu.VMEM((count, feat), F32)],
            compiler_params=params(),
            cost_estimate=cost(4 * count * feat * hidden, 4 * feat * hidden),
            name="back",
        )(*args)
        outs = list(outs)
        own_now = outs.pop(0) if has_own else None
        cot_now = outs.pop(0)
        q = outs.pop(0) if keep else None
        return own_now, cot_now, q, outs

    count = len(chunks)
    kept = [None] * count
    recv, base, own_recv = first_recv, sent, None
    prev = [None] * count
    acc = jnp.zeros((-(-(experts + 1) // 8) * 8, feat), F32)
    up_spec = pl.BlockSpec((feat, width), lambda i: (0, i))
    down_spec = pl.BlockSpec((width, feat), lambda i: (i, 0))
    for stage in range(sections):
        parts, qs, cots = {}, [], []
        after = None
        for index, chunk in enumerate(chunks):
            if stage == 0:
                first = index == 0
                kept[index] = forward(chunk, gather_next if first else after, down_far if first else None)
                if first:
                    down_near = kept[index].pop()
                after = None
            own_now, cot_now, q, outs = back(
                stage, chunk, kept[index][0], kept[index][1], recv, base, own_recv, own, prev[index], after
            )
            if chunk[0] == 0:
                own = own_now
            cots.append(cot_now)
            qs.append(q)
            parts.update(zip(chunk, outs))
            after = outs[0]
        prev = cots
        section = last - stage
        partial = [parts[0]] + [spread(parts[step], -step, [section], 0) for step in steps[1:]]
        want_next = section > 0
        if want_next:
            extra, extra_specs = [], []
        else:
            up_grad, mark = pl.pallas_call(
                functools.partial(up_kernel, count),
                grid=(blocks,),
                out_shape=[sds((feat, hidden)), sds((8, 128), F32)],
                in_specs=[const((chunk_rows(c), feat)) for c in chunks] + [col_block(c) for c in chunks],
                out_specs=[up_spec, const((8, 128))],
                scratch_shapes=[pltpu.VMEM((feat, chunk_rows(c)), BF16) for c in chunks],
                compiler_params=params(),
                cost_estimate=cost(2 * shards * slots * feat * hidden, 2 * feat * hidden),
                name="up_grad",
            )(*[k[2] for k in kept], *qs)
            extra, extra_specs = [mark], [any_place()]
        outs = pl.pallas_call(
            functools.partial(owner_kernel, shards, slices, slots, stage, want_next),
            out_shape=[sds(acc.shape, F32)]
            + ([sds((total, feat))] + [sds((slots, feat))] * (shards - 1) if want_next else []),
            in_specs=[smem()] + extra_specs + [vmem()] * (shards + 7 + (1 if want_next else 0)),
            out_specs=[vmem()] * (1 + (shards if want_next else 0)),
            compiler_params=params(),
            cost_estimate=cost(1e7, 4e6),
            name="owner",
        )(place, *extra, *partial, own, x, gain, router, score, scatter, acc, *([gather_next] if want_next else []))
        acc = outs[0]
        if want_next:
            own_recv = spread(outs[1], 0, [section], 1)
            recv = [None] + [spread(outs[1 + step], step, [section], 1) for step in steps[1:]]
            base = 0
    sums = [acc] + [spread(acc, step, everyone, 0) for step in steps[1:]]
    down_grad = pl.pallas_call(
        functools.partial(down_kernel, count),
        grid=(blocks,),
        out_shape=sds((hidden, feat)),
        in_specs=[any_place()]
        + [const((chunk_rows(c), feat)) for c in chunks]
        + [const((chunk_rows(c), 1)) for c in chunks]
        + [col_block(c) for c in chunks],
        out_specs=down_spec,
        scratch_shapes=[pltpu.VMEM((chunk_rows(c), feat), BF16) for c in chunks],
        compiler_params=params(),
        cost_estimate=cost(2 * shards * slots * feat * hidden, 2 * feat * hidden),
        name="down_grad",
    )(acc, *cots, *[k[3] for k in kept], *[k[0] for k in kept])
    router_grad, gain_grad = pl.pallas_call(
        functools.partial(finish_kernel, shards, experts),
        out_shape=[sds((experts, feat), F32), sds((1, feat), F32)],
        in_specs=[vmem()] * shards,
        out_specs=[vmem()] * 2,
        compiler_params=params(),
        name="finish",
    )(*sums)
    return (up_grad[None], down_grad[None], router_grad[None], gain_grad)


def solution(mesh):
    in_specs = (
        P("section", None, ("groups", "expert"), None),
        P(None, ("groups", "expert"), None),
        P("section", None, "groups", None),
        P("section", None),
        P("section", None, None),
        P("section", None, "expert"),
        P("section", "expert", None),
    )
    out_specs = (
        P("section", "groups", "expert"),
        P("section", "expert", "groups"),
        P("section", "groups", None),
        P("section", "groups"),
    )
    return jax.shard_map(body, mesh=mesh, in_specs=in_specs, out_specs=out_specs, check_vma=False)
```

```python
import functools

import jax
import jax.numpy as jnp
from jax import lax
from jax.experimental import pallas as pl
from jax.experimental.pallas import tpu as pltpu
from jax.sharding import PartitionSpec as P

norm_eps = 1e-06
gelu_coef = 0.7978845608028654
cubic_coef = 0.044715
BLOCK_ROWS = 64
BLOCK_CAP = 40
F32 = jnp.float32
BF16 = jnp.bfloat16
AUX = 8
SIDES = 4
FEAT_WIDTH = 512


def vmem():
    return pl.BlockSpec(memory_space=pltpu.VMEM)


def smem():
    return pl.BlockSpec(memory_space=pltpu.SMEM)


def params(mebi=12):
    return pltpu.CompilerParams(vmem_limit_bytes=mebi * 1024 * 1024)


def cost(flops, nbytes):
    return pl.CostEstimate(flops=int(flops), bytes_accessed=int(nbytes), transcendentals=0)


def dot(a, b, dims):
    return lax.dot_general(a, b, ((dims[0:1], dims[1:2]), ((), ())), preferred_element_type=F32)


def iota(shape, dim):
    return lax.broadcasted_iota(jnp.int32, shape, dim)


def row_norm(values):
    mean_sq = jnp.mean(values * values, axis=-1, keepdims=True)
    return lax.rsqrt(mean_sq + norm_eps)


def eye(size):
    return (iota((size, size), 0) == iota((size, size), 1)).astype(F32)


def prep_kernel(
    shards, slices, rows, slots, cap, place, x_far, cot_far, gain_far, router_far, col_ref, row_ref, *outs
):
    x_ref, cot_ref, gain_ref, router_ref, sems = outs[-5:]
    outs = outs[:-5]
    loads = [
        pltpu.make_async_copy(source, target, sems.at[index])
        for index, (source, target) in enumerate([(x_far, x_ref), (cot_far, cot_ref), (gain_far, gain_ref), (router_far, router_ref)])
    ]
    for load in loads:
        load.start()
    for load in loads:
        load.wait()
    h_outs, c_outs = outs[:shards], outs[shards : 2 * shards - 1]
    gather_ref, scatter_ref, score_ref, own_ref = outs[2 * shards - 1 :]
    me = place[0]
    is_last = place[1] == place[2]
    total = x_ref.shape[0]
    experts = router_ref.shape[0]
    x = x_ref[...].astype(F32)
    h32 = (x * row_norm(x)) * gain_ref[...]
    h = h32.astype(BF16)
    logits = lax.dot_general(
        h.astype(F32), router_ref[...], (((1,), (1,)), ((), ())),
        preferred_element_type=F32, precision=lax.Precision.HIGHEST,
    )
    scores = 1.0 / (1.0 + jnp.exp(-logits))
    ids = iota((total, experts), 1)
    hits = jnp.logical_or(col_ref[:, 0:1] == ids, col_ref[:, 1:2] == ids).astype(F32)
    totals = jnp.sum(scores * hits, axis=-1, keepdims=True)
    weights = scores * hits / totals
    slopes = scores * (1.0 - scores) / totals
    score_ref[0] = scores
    score_ref[1] = weights
    score_ref[2] = hits
    score_ref[3] = jnp.broadcast_to(totals, (total, experts))
    first, second = iota((total, total), 0), iota((total, total), 1)
    same = (first // rows) == (second // rows)
    before = jnp.logical_and(same, second < first).astype(BF16)
    after = jnp.logical_and(same, first < second).astype(BF16)
    base_col = (iota((total, experts), 0) // rows * cap).astype(F32)
    slot_col = jnp.where(hits > 0.0, dot(before, hits.astype(BF16), (1, 0)) + base_col, -1.0)
    ids_row = iota((experts, total), 0)
    hits_row = jnp.logical_or(row_ref[0:1, :] == ids_row, row_ref[1:2, :] == ids_row).astype(F32)
    base_row = (iota((experts, total), 1) // rows * cap).astype(F32)
    slot_row = jnp.where(hits_row > 0.0, dot(hits_row.astype(BF16), after, (1, 0)) + base_row, -1.0)
    cot = cot_ref[...]
    own_ref[...] = jnp.where(is_last, cot.astype(F32), 0.0).astype(BF16)
    slot_lane = iota((total, slots), 1).astype(F32)
    slot_sub = iota((slots, total), 0).astype(F32)
    for step in range(shards):
        expert = lax.rem(me + step, shards) // slices
        mine = (ids == expert).astype(F32)
        slot_c = jnp.sum(slot_col * mine, axis=-1, keepdims=True)
        slot_r = jnp.sum(slot_row * (ids_row == expert).astype(F32), axis=0, keepdims=True)
        scatter = (slot_c == slot_lane).astype(F32)
        gather = (slot_r == slot_sub).astype(F32).astype(BF16)
        weight_c = jnp.sum(weights * mine, axis=-1, keepdims=True)
        rest = hits * (1.0 - mine)
        slope_c = jnp.sum(slopes * mine, axis=-1, keepdims=True)
        slope_o = jnp.sum(slopes * rest, axis=-1, keepdims=True)
        other_c = jnp.sum(ids.astype(F32) * rest, axis=-1, keepdims=True)
        sides = [weight_c, (1.0 - weight_c) * slope_c, 0.0 - weight_c * slope_o, other_c]
        aux = jnp.zeros((AUX, slots), F32)
        aux_id = iota((AUX, slots), 0)
        for index, side in enumerate(sides):
            side_r = jnp.sum(scatter * side, axis=0, keepdims=True)
            high = side_r.astype(BF16).astype(F32)
            aux = jnp.where(aux_id == 2 * index, high, jnp.where(aux_id == 2 * index + 1, side_r - high, aux))
        aux = aux.astype(BF16)
        picked = dot(gather, h, (1, 0)).astype(BF16)
        for target in [h_outs[step]] + ([c_outs[step - 1]] if step else []):
            target[0:slots, :] = picked
            target[slots : slots + AUX, :] = jnp.zeros((AUX, x.shape[1]), BF16)
            target[slots : slots + AUX, 0:slots] = aux
        if step:
            c_outs[step - 1][slots + AUX :, :] = dot(gather, cot, (1, 0)).astype(BF16)
        gather_ref[step] = gather
        scatter_ref[step] = scatter.astype(BF16)


def forward_kernel(slots, width, loads, own, others, *refs):
    refs = list(refs)[1:]
    take = lambda n: [refs.pop(0) for _ in range(n)]
    sources = [take(1) for _ in range(own)] + [take(2) for _ in range(others)]
    far = take(2 if loads else 0)
    near = take(0 if loads else 1)
    act_ref, slope_ref, rows_ref, side_ref = take(4)
    if loads:
        near = take(2)
        sems = refs[0]
    up_ref = near[0]
    blocks = up_ref.shape[1] // width

    def column_load(index):
        span = pl.ds(pl.multiple_of(index * width, width), width)
        return pltpu.make_async_copy(far[0].at[:, span], up_ref.at[:, span], sems.at[index])

    if loads:
        for index in range(blocks):
            column_load(index).start()
        down_load = pltpu.make_async_copy(far[1], near[1], sems.at[blocks])
        down_load.start()
    for index, source in enumerate(sources):
        span = slice(index * slots, (index + 1) * slots)
        value = source[0][0 : slots + AUX, :].astype(F32)
        for extra in source[1:]:
            value = value + extra[0 : slots + AUX, :].astype(F32)
        rows_ref[span, :] = value[0:slots, :].astype(BF16)
        for column in range(SIDES):
            low = slots + 2 * column
            side_r = value[low : low + 1, 0:slots] + value[low + 1 : low + 2, 0:slots]
            side_ref[span, column : column + 1] = jnp.sum(eye(slots) * side_r, axis=-1, keepdims=True)

    def block(index, carry):
        if loads:
            column_load(index).wait()
        span = pl.ds(pl.multiple_of(index * width, width), width)
        u = dot(rows_ref[...], up_ref[:, span], (1, 0))
        square = u * u
        tanh_val = jnp.tanh(gelu_coef * (u + cubic_coef * square * u))
        half = 0.5 * (1.0 + tanh_val)
        act_ref[:, span] = (u * half).astype(BF16)
        slope = half + 0.5 * u * (1.0 - tanh_val * tanh_val) * (gelu_coef * (1.0 + 3.0 * cubic_coef * square))
        slope_ref[:, span] = (slope * side_ref[:, 0:1]).astype(BF16)
        return carry

    lax.fori_loop(0, blocks, block, 0)
    if loads:
        down_load.wait()


def back_kernel(shards, slices, slots, width, base, stage, keep, has_prev, spans, place, *refs):
    refs = list(refs)
    take = lambda n: [refs.pop(0) for _ in range(n)]
    reached = place[1] + stage >= place[2]
    own_in = take(2 if has_prev else 1)
    gather_ref = take(1)[0]
    recv_in = take(shards - 1)
    prev_ref = take(1)[0] if has_prev else None
    up_ref, down_ref = take(2)
    act_refs, slope_refs = take(len(spans)), take(len(spans))
    row_refs, side_refs = (take(len(spans)), take(len(spans))) if keep else ([], [])
    gain_ref, router_ref = take(2) if keep else (None, None)
    own_out = None if keep else take(1)[0]
    cot_ref = take(1)[0]
    q_refs = take(len(spans)) if keep else []
    acc_ref = take(1)[0] if keep else None
    parts = [] if keep else take(shards)
    q_ref = refs[0]
    own = own_in[0][...]
    if has_prev:
        own = (own.astype(F32) + own_in[1][...].astype(F32)).astype(BF16)
    if not keep:
        own_out[...] = own
    cot_ref[0:slots, :] = dot(gather_ref[0], own, (1, 0)).astype(BF16)
    for place_at in range(1, shards):
        rows = slice(place_at * slots, (place_at + 1) * slots)
        value = recv_in[place_at - 1][base : base + slots, :]
        if has_prev:
            value = (value.astype(F32) + prev_ref[rows, :].astype(F32)).astype(BF16)
        cot_ref[rows, :] = value

    @pl.when(reached)
    def _():
        hidden, feat = down_ref.shape
        lanes = 128

        def block(index, combs):
            span = pl.ds(pl.multiple_of(index * width, width), width)
            t_all = dot(cot_ref[...], down_ref[span, :], (1, 1))
            out = []
            for which, (low, high) in enumerate(spans):
                t = t_all[low:high, :]
                prod = act_refs[which][:, span].astype(F32) * t
                comb = combs[which]
                for start in range(0, width, lanes):
                    comb = comb + prod[:, start : start + lanes]
                out.append(comb)
                q = (slope_refs[which][:, span].astype(F32) * t).astype(BF16)
                q_ref[low:high, span] = q
                if keep:
                    q_refs[which][:, span] = q
            return tuple(out)

        combs = lax.fori_loop(
            0, hidden // width, block, tuple(jnp.zeros((high - low, lanes), F32) for low, high in spans)
        )
        wide = min(FEAT_WIDTH, feat)
        if keep:
            experts = router_ref.shape[0]
            expert = place[0] // slices
            acc_ref[...] = jnp.zeros_like(acc_ref)
            routed = jnp.zeros((experts, feat), F32)
            for which, (low, high) in enumerate(spans):
                comb_c = jnp.sum(combs[which], axis=-1, keepdims=True)
                ids = iota((high - low, experts), 1)
                other = side_refs[which][:, 3:4]
                pull = jnp.where(ids == expert, comb_c * side_refs[which][:, 1:2], 0.0)
                pull = pull + jnp.where(ids.astype(F32) == other, comb_c * side_refs[which][:, 2:3], 0.0)
                routed = routed + lax.dot_general(
                    pull, row_refs[which][...].astype(F32), (((0,), (0,)), ((), ())),
                    preferred_element_type=F32, precision=lax.Precision.HIGHEST,
                )
            acc_ref[0:experts, :] = routed
        for start in range(0, feat, wide):
            cols = slice(start, start + wide)
            term = dot(q_ref[...], up_ref[cols, :], (1, 1))
            if keep:
                gained = jnp.sum(routed[:, cols] * router_ref[:, cols], axis=0, keepdims=True)
                for which, (low, high) in enumerate(spans):
                    rows = row_refs[which][:, cols].astype(F32)
                    gained = gained + jnp.sum(term[low:high, :] * rows, axis=0, keepdims=True)
                acc_ref[experts : experts + 1, cols] = gained / gain_ref[:, cols]
            for index, part in enumerate(parts):
                part[0:slots, cols] = term[index * slots : (index + 1) * slots, :].astype(BF16)
        for which, (low, high) in enumerate([] if keep else spans):
            comb_c = jnp.sum(combs[which], axis=-1, keepdims=True)
            for index in range(low // slots, high // slots):
                part = parts[index]
                mine = comb_c[index * slots - low : (index + 1) * slots - low, :]
                comb_r = jnp.sum(eye(slots) * mine, axis=0, keepdims=True)
                part[slots : slots + AUX, :] = jnp.zeros((AUX, feat), BF16)
                part[slots : slots + AUX, 0:slots] = jnp.broadcast_to(comb_r, (AUX, slots)).astype(BF16)


def owner_kernel(shards, slices, slots, stage, place, *refs):
    parts = refs[:shards]
    own_ref, x_ref, gain_ref, router_ref, score_ref, scatter_ref, gather_ref = refs[shards : shards + 7]
    own_out, sends = refs[shards + 7], refs[shards + 8 :]
    me = place[0]

    @pl.when(place[1] == place[2] - stage)
    def _():
        experts = router_ref.shape[0]
        total = x_ref.shape[0]
        ids = iota((total, experts), 1)
        gh = jnp.zeros(x_ref.shape, F32)
        comb = jnp.zeros((total, experts), F32)
        for step in range(shards):
            expert = lax.rem(me + step, shards) // slices
            scatter = scatter_ref[step]
            gh = gh + dot(scatter, parts[step][0:slots, :], (1, 0))
            comb_r = parts[step][slots : slots + AUX, 0:slots].astype(F32)[0:1, :]
            comb_c = jnp.sum(scatter.astype(F32) * comb_r, axis=-1, keepdims=True)
            comb = comb + comb_c * (ids == expert).astype(F32)
        scores, weights, hits, totals = (score_ref[i] for i in range(4))
        center_comb = jnp.sum(weights * comb, axis=-1, keepdims=True)
        logit_grad = hits * (comb - center_comb) / totals * (scores * (1.0 - scores))
        for expert in range(experts):
            gh = gh + logit_grad[:, expert : expert + 1] * router_ref[expert : expert + 1, :]
        x = x_ref[...].astype(F32)
        inverse = row_norm(x)
        normed = x * inverse
        scaled = gh * gain_ref[...]
        center = jnp.mean(scaled * normed, axis=-1, keepdims=True)
        gx = (own_ref[...].astype(F32) + inverse * (scaled - normed * center)).astype(BF16)
        own_out[...] = gx
        for step in range(1, shards):
            sends[step - 1][...] = dot(gather_ref[step], gx, (1, 0)).astype(BF16)


def up_kernel(count, *refs):
    rows, qs = refs[:count], refs[count : 2 * count]
    out_ref = refs[2 * count]
    turned = refs[2 * count + 1 :]

    @pl.when(pl.program_id(0) == 0)
    def _():
        for index in range(count):
            turned[index][...] = rows[index][...].astype(F32).T.astype(BF16)

    total = dot(turned[0][...], qs[0][...], (1, 0))
    for index in range(1, count):
        total = total + dot(turned[index][...], qs[index][...], (1, 0))
    out_ref[...] = total.astype(BF16)


def down_kernel(spans, cot_ref, *refs):
    count = len(spans)
    sides, acts = (refs[i * count : (i + 1) * count] for i in range(2))
    out_ref = refs[2 * count]
    y_refs = refs[2 * count + 1 :]

    @pl.when(pl.program_id(0) == 0)
    def _():
        for index in range(count):
            cots = cot_ref[spans[index][0] : spans[index][1], :].astype(F32)
            y_refs[index][...] = (sides[index][:, 0:1] * cots).astype(BF16)

    total = dot(acts[0][...], y_refs[0][...], (0, 0))
    for index in range(1, count):
        total = total + dot(acts[index][...], y_refs[index][...], (0, 0))
    out_ref[...] = total.astype(BF16)


def finish_kernel(shards, experts, *refs):
    total = refs[0][...]
    for ref in refs[1:shards]:
        total = total + ref[...]
    refs[shards][...] = total[0:experts, :]
    refs[shards + 1][...] = total[experts : experts + 1, :]


def body(
    layer_inputs, out_cotangent, expert_routes, norm_gain, router_weight, up_weight, down_weight
):
    sections = lax.axis_size("section")
    section_id = lax.axis_index("section")
    shards = lax.axis_size("expert")
    shard_id = lax.axis_index("expert")
    micro, rows, feat = layer_inputs.shape[1:]
    router = router_weight[0]
    experts = router.shape[0]
    up = up_weight[0]
    down = down_weight[0]
    hidden = up.shape[1]
    slices = shards // experts
    total = micro * rows
    cap = rows // BLOCK_ROWS * BLOCK_CAP if rows % BLOCK_ROWS == 0 else rows
    slots = micro * cap
    sent = slots + AUX
    last = sections - 1
    x = layer_inputs[0].reshape(total, feat)
    cot = out_cotangent.reshape(total, feat)
    chosen = lax.dynamic_slice_in_dim(expert_routes[0], shard_id * rows, rows, 1).reshape(total, 2)
    gain = norm_gain
    place = jnp.stack([shard_id, section_id, jnp.int32(last)]).astype(jnp.int32)
    steps = list(range(shards))
    split = max(1, shards // 2)
    chunks = [steps[:split], steps[split:]]
    chunks = [chunk for chunk in chunks if chunk]
    width = min(1024, hidden)
    blocks = hidden // width

    def sds(shape, dtype=BF16):
        return jax.ShapeDtypeStruct(shape, dtype)

    def move(value, pairs):
        flat = [(sz * sections + ss, dz * sections + ds) for (ss, sz), (ds, dz) in pairs]
        return lax.ppermute(value, ("expert", "section"), flat)

    def spread(value, step, sources, drop):
        return move(
            value,
            [((s, z), (s - drop, (z + step) % shards)) for s in sources for z in range(shards) if s - drop >= 0],
        )

    def any_place():
        return pl.BlockSpec(memory_space=pl.ANY)

    everyone = list(range(sections))
    far = [pltpu.with_memory_space_constraint(array, pltpu.HBM) for array in (x, cot, gain, router, up, down)]
    hbm = pl.BlockSpec(memory_space=pltpu.HBM)
    prep = pl.pallas_call(
        functools.partial(prep_kernel, shards, slices, rows, slots, cap),
        out_shape=[sds((sent, feat))] * shards
        + [sds((sent + slots, feat))] * (shards - 1)
        + [sds((shards, slots, total)), sds((shards, total, slots)), sds((4, total, experts), F32), sds((total, feat))],
        in_specs=[smem()] + [hbm] * 4 + [vmem()] * 2,
        out_specs=[vmem()] * (2 * shards + 3),
        scratch_shapes=[pltpu.VMEM((total, feat), BF16)] * 2
        + [pltpu.VMEM(gain.shape, F32), pltpu.VMEM(router.shape, F32), pltpu.SemaphoreType.DMA((4,))],
        compiler_params=params(),
        cost_estimate=cost(1e7, 4e6),
        name="prep",
    )(place, *far[:4], chosen, chosen.T)
    h_send, c_send = prep[:shards], [None] + list(prep[shards : 2 * shards - 1])
    gather, scatter, score, own = prep[2 * shards - 1 :]
    first_recv = [None] + [spread(c_send[step], step, [last], 0) for step in steps[1:]]
    h_recv = [None] + [spread(h_send[step], step, everyone[:-1], 0) for step in steps[1:]]
    gather_next = move(gather, [((s - 1, z), (s, z)) for s in everyone[1:] for z in range(shards)])
    def const(block):
        return pl.BlockSpec(block, lambda i: (0,) * len(block))

    def chunk_rows(chunk):
        return len(chunk) * slots

    def col_block(chunk):
        return pl.BlockSpec((chunk_rows(chunk), width), lambda i: (0, i))

    def forward(chunk, after, near):
        count = chunk_rows(chunk)
        own_part = 1 if chunk[0] == 0 else 0
        args = [after] + [h_send[0]] * own_part
        for step in chunk[own_part:]:
            args += [first_recv[step], h_recv[step]]
        specs = [any_place()] + [vmem()] * (len(args) - 1)
        args += [near[0]] if near else far[4:]
        specs += [vmem()] if near else [hbm] * 2
        return pl.pallas_call(
            functools.partial(forward_kernel, slots, width, not near, own_part, len(chunk) - own_part),
            out_shape=[sds((count, hidden))] * 2
            + [sds((count, feat)), sds((count, SIDES), F32)]
            + ([] if near else [pltpu.VMEM(up.shape, BF16), pltpu.VMEM(down.shape, BF16)]),
            in_specs=specs,
            out_specs=[vmem()] * (4 if near else 6),
            scratch_shapes=[] if near else [pltpu.SemaphoreType.DMA((blocks + 1,))],
            compiler_params=params(),
            cost_estimate=cost(2 * count * feat * hidden, 2 * feat * hidden),
            name="forward",
        )(*args)

    def back(stage, recv, base, own_recv, own, prev):
        has_prev = prev is not None
        keep = stage == last
        args = [place] + ([own_recv, own] if has_prev else [own]) + [gather]
        args += [recv[step] for step in steps[1:]]
        if has_prev:
            args += [prev]
        args += near + [k[0] for k in kept] + [k[1] for k in kept]
        if keep:
            args += [k[2] for k in kept] + [k[3] for k in kept] + [gain, router]
        every = shards * slots
        outs = pl.pallas_call(
            functools.partial(back_kernel, shards, slices, slots, width, base, stage, keep, has_prev, spans),
            out_shape=([] if keep else [sds((total, feat))])
            + [sds((every, feat))]
            + ([sds((chunk_rows(chunk), hidden)) for chunk in chunks] if keep else [])
            + ([sds((-(-(experts + 1) // 8) * 8, feat), F32)] if keep else [sds((sent, feat))] * shards),
            in_specs=[smem()] + [vmem()] * (len(args) - 1),
            out_specs=[vmem()] * (2 + len(chunks) if keep else 2 + shards),
            scratch_shapes=[pltpu.VMEM((every, hidden), BF16)],
            compiler_params=params(),
            cost_estimate=cost(4 * every * feat * hidden, 4 * feat * hidden),
            name="back",
        )(*args)
        return list(outs)

    spans = [(chunk[0] * slots, (chunk[-1] + 1) * slots) for chunk in chunks]
    count = len(chunks)
    kept, near = [], []
    after = gather_next
    for chunk in chunks:
        outs = forward(chunk, after, near)
        kept.append(outs[:4])
        after = outs[3]
        if not near:
            near = [pltpu.with_memory_space_constraint(array, pltpu.VMEM) for array in outs[4:]]
    recv, base, own_recv, prev = first_recv, sent, None, None
    for stage in range(last):
        own, prev, *parts = back(stage, recv, base, own_recv, own, prev)
        section = last - stage
        partial = [parts[0]] + [spread(parts[step], -step, [section], 0) for step in steps[1:]]
        outs = pl.pallas_call(
            functools.partial(owner_kernel, shards, slices, slots, stage),
            out_shape=[sds((total, feat))] + [sds((slots, feat))] * (shards - 1),
            in_specs=[smem()] + [vmem()] * (shards + 7),
            out_specs=[vmem()] * shards,
            compiler_params=params(),
            cost_estimate=cost(1e7, 4e6),
            name="owner",
        )(place, *partial, own, x, gain, router, score, scatter, gather_next)
        own_recv = spread(outs[0], 0, [section], 1)
        recv = [None] + [spread(outs[step], step, [section], 1) for step in steps[1:]]
        base = 0
    cots, *qs, acc = back(last, recv, base, own_recv, own, prev)
    sums = [acc] + [spread(acc, step, everyone, 0) for step in steps[1:]]
    up_grad = pl.pallas_call(
        functools.partial(up_kernel, count),
        grid=(blocks,),
        out_shape=sds((feat, hidden)),
        in_specs=[const((chunk_rows(c), feat)) for c in chunks] + [col_block(c) for c in chunks],
        out_specs=pl.BlockSpec((feat, width), lambda i: (0, i)),
        scratch_shapes=[pltpu.VMEM((feat, chunk_rows(c)), BF16) for c in chunks],
        compiler_params=params(24),
        cost_estimate=cost(2 * shards * slots * feat * hidden, 2 * feat * hidden),
        name="up_grad",
    )(*[k[2] for k in kept], *qs)
    down_grad = pl.pallas_call(
        functools.partial(down_kernel, spans),
        grid=(blocks,),
        out_shape=sds((hidden, feat)),
        in_specs=[const(cots.shape)]
        + [const((chunk_rows(c), SIDES)) for c in chunks]
        + [col_block(c) for c in chunks],
        out_specs=pl.BlockSpec((width, feat), lambda i: (i, 0)),
        scratch_shapes=[pltpu.VMEM((chunk_rows(c), feat), BF16) for c in chunks],
        compiler_params=params(24),
        cost_estimate=cost(2 * shards * slots * feat * hidden, 2 * feat * hidden),
        name="down_grad",
    )(cots, *[k[3] for k in kept], *[k[0] for k in kept])
    router_grad, gain_grad = pl.pallas_call(
        functools.partial(finish_kernel, shards, experts),
        out_shape=[sds((experts, feat), F32), sds((1, feat), F32)],
        in_specs=[vmem()] * shards,
        out_specs=[vmem()] * 2,
        compiler_params=params(),
        name="finish",
    )(*sums)
    return (up_grad[None], down_grad[None], router_grad[None], gain_grad)


def solution(mesh):
    in_specs = (
        P("section", None, ("groups", "expert"), None),
        P(None, ("groups", "expert"), None),
        P("section", None, "groups", None),
        P("section", None),
        P("section", None, None),
        P("section", None, "expert"),
        P("section", "expert", None),
    )
    out_specs = (
        P("section", "groups", "expert"),
        P("section", "expert", "groups"),
        P("section", "groups", None),
        P("section", "groups"),
    )
    return jax.shard_map(body, mesh=mesh, in_specs=in_specs, out_specs=out_specs, check_vma=False)
```

```python
import functools

import jax
import jax.numpy as jnp
from jax import lax
from jax.experimental import pallas as pl
from jax.experimental.pallas import tpu as pltpu
from jax.sharding import PartitionSpec as P


norm_eps = 1e-06
gelu_coef = 0.7978845608028654
cubic_coef = 0.044715
BLOCK_ROWS = 64
BLOCK_CAP = 40
F32 = jnp.float32
BF16 = jnp.bfloat16
AUX = 8
SIDES = 4
FEAT_WIDTH = 512
GRAD_WIDTH = 1024


def vmem():
    return pl.BlockSpec(memory_space=pltpu.VMEM)


def smem():
    return pl.BlockSpec(memory_space=pltpu.SMEM)


def params(mebi=12):
    return pltpu.CompilerParams(vmem_limit_bytes=mebi * 1024 * 1024)


def cost(flops, nbytes):
    return pl.CostEstimate(flops=int(flops), bytes_accessed=int(nbytes), transcendentals=0)


def dot(a, b, dims):
    return lax.dot_general(a, b, ((dims[0:1], dims[1:2]), ((), ())), preferred_element_type=F32)


def iota(shape, dim):
    return lax.broadcasted_iota(jnp.int32, shape, dim)


def row_norm(values):
    mean_sq = jnp.mean(values * values, axis=-1, keepdims=True)
    return lax.rsqrt(mean_sq + norm_eps)


def eye(size):
    return (iota((size, size), 0) == iota((size, size), 1)).astype(F32)


def prep_kernel(
    shards, slices, rows, slots, cap, place, x_far, cot_far, gain_far, router_far, col_ref, row_ref, *outs
):
    x_ref, cot_ref, gain_ref, router_ref, sems = outs[-5:]
    outs = outs[:-5]
    loads = [
        pltpu.make_async_copy(source, target, sems.at[index])
        for index, (source, target) in enumerate([(x_far, x_ref), (cot_far, cot_ref), (gain_far, gain_ref), (router_far, router_ref)])
    ]
    for load in loads:
        load.start()
    for load in loads:
        load.wait()
    h_outs, c_outs = outs[:shards], outs[shards : 2 * shards - 1]
    gather_ref, scatter_ref, own_ref = outs[2 * shards - 1 :]
    me = place[0]
    is_last = place[1] == place[2]
    total = x_ref.shape[0]
    experts = router_ref.shape[0]
    x = x_ref[...].astype(F32)
    h32 = (x * row_norm(x)) * gain_ref[...]
    h = h32.astype(BF16)
    logits = lax.dot_general(
        h.astype(F32), router_ref[...], (((1,), (1,)), ((), ())),
        preferred_element_type=F32, precision=lax.Precision.HIGHEST,
    )
    scores = 1.0 / (1.0 + jnp.exp(-logits))
    ids = iota((total, experts), 1)
    hits = jnp.logical_or(col_ref[:, 0:1] == ids, col_ref[:, 1:2] == ids).astype(F32)
    totals = jnp.sum(scores * hits, axis=-1, keepdims=True)
    weights = scores * hits / totals
    slopes = scores * (1.0 - scores) / totals
    first, second = iota((total, total), 0), iota((total, total), 1)
    same = (first // rows) == (second // rows)
    before = jnp.logical_and(same, second < first).astype(BF16)
    after = jnp.logical_and(same, first < second).astype(BF16)
    base_col = (iota((total, experts), 0) // rows * cap).astype(F32)
    slot_col = jnp.where(hits > 0.0, dot(before, hits.astype(BF16), (1, 0)) + base_col, -1.0)
    ids_row = iota((experts, total), 0)
    hits_row = jnp.logical_or(row_ref[0:1, :] == ids_row, row_ref[1:2, :] == ids_row).astype(F32)
    base_row = (iota((experts, total), 1) // rows * cap).astype(F32)
    slot_row = jnp.where(hits_row > 0.0, dot(hits_row.astype(BF16), after, (1, 0)) + base_row, -1.0)
    cot = cot_ref[...]
    own_ref[...] = jnp.where(is_last, cot.astype(F32), 0.0).astype(BF16)
    slot_lane = iota((total, slots), 1).astype(F32)
    slot_sub = iota((slots, total), 0).astype(F32)
    for step in range(shards):
        expert = lax.rem(me + step, shards) // slices
        mine = (ids == expert).astype(F32)
        slot_c = jnp.sum(slot_col * mine, axis=-1, keepdims=True)
        slot_r = jnp.sum(slot_row * (ids_row == expert).astype(F32), axis=0, keepdims=True)
        scatter = (slot_c == slot_lane).astype(F32)
        gather = (slot_r == slot_sub).astype(F32).astype(BF16)
        weight_c = jnp.sum(weights * mine, axis=-1, keepdims=True)
        rest = hits * (1.0 - mine)
        slope_c = jnp.sum(slopes * mine, axis=-1, keepdims=True)
        slope_o = jnp.sum(slopes * rest, axis=-1, keepdims=True)
        other_c = jnp.sum(ids.astype(F32) * rest, axis=-1, keepdims=True)
        sides = [weight_c, (1.0 - weight_c) * slope_c, 0.0 - weight_c * slope_o, other_c]
        aux = jnp.zeros((AUX, slots), F32)
        aux_id = iota((AUX, slots), 0)
        for index, side in enumerate(sides):
            side_r = jnp.sum(scatter * side, axis=0, keepdims=True)
            high = side_r.astype(BF16).astype(F32)
            aux = jnp.where(aux_id == 2 * index, high, jnp.where(aux_id == 2 * index + 1, side_r - high, aux))
        aux = aux.astype(BF16)
        picked = dot(gather, h, (1, 0)).astype(BF16)
        for target in [h_outs[step]] + ([c_outs[step - 1]] if step else []):
            target[0:slots, :] = picked
            target[slots : slots + AUX, :] = jnp.zeros((AUX, x.shape[1]), BF16)
            target[slots : slots + AUX, 0:slots] = aux
        if step:
            c_outs[step - 1][slots + AUX :, :] = dot(gather, cot, (1, 0)).astype(BF16)
        gather_ref[step] = gather
        scatter_ref[step] = scatter.astype(BF16)


def forward_rows(sources, slots, row0, up_ref, width, outs, ready):
    act_ref, slope_ref, rows_ref, side_ref = outs
    count = len(sources) * slots
    for index, source in enumerate(sources):
        span = slice(row0 + index * slots, row0 + (index + 1) * slots)
        value = source[0 : slots + AUX, :].astype(F32)
        rows_ref[span, :] = value[0:slots, :].astype(BF16)
        for column in range(SIDES):
            low = slots + 2 * column
            side_r = value[low : low + 1, 0:slots] + value[low + 1 : low + 2, 0:slots]
            side_ref[span, column : column + 1] = jnp.sum(eye(slots) * side_r, axis=-1, keepdims=True)
    rows = slice(row0, row0 + count)

    def block(index, carry):
        ready(index)
        span = pl.ds(pl.multiple_of(index * width, width), width)
        u = dot(rows_ref[rows, :], up_ref[:, span], (1, 0))
        square = u * u
        tanh_val = jnp.tanh(gelu_coef * (u + cubic_coef * square * u))
        half = 0.5 * (1.0 + tanh_val)
        act_ref[rows, span] = (u * half).astype(BF16)
        slope = half + 0.5 * u * (1.0 - tanh_val * tanh_val) * (gelu_coef * (1.0 + 3.0 * cubic_coef * square))
        slope_ref[rows, span] = (slope * side_ref[rows, 0:1]).astype(BF16)
        return carry

    lax.fori_loop(0, up_ref.shape[1] // width, block, 0)


def first_kernel(slots, width, parts, place, *refs):
    sources = refs[:parts]
    up_far, down_far = refs[parts : parts + 2]
    outs = refs[parts + 2 : parts + 6]
    up_ref, down_ref, sems = refs[parts + 6 :]
    blocks = up_ref.shape[1] // width
    last = place[1] == place[2]

    def column_load(index):
        span = pl.ds(pl.multiple_of(index * width, width), width)
        return pltpu.make_async_copy(up_far.at[:, span], up_ref.at[:, span], sems.at[index])

    down_load = pltpu.make_async_copy(down_far, down_ref, sems.at[blocks])
    for index in range(blocks):
        column_load(index).start()
    down_load.start()

    @pl.when(last)
    def _():
        forward_rows(sources, slots, 0, up_ref, width, outs, lambda index: column_load(index).wait())

    @pl.when(jnp.logical_not(last))
    def _():
        for index in range(blocks):
            column_load(index).wait()

    down_load.wait()


def second_kernel(slots, width, parts, place, *refs):
    sources = refs[:parts]
    refs = refs[:parts] + refs[parts + 1 :]
    before = refs[parts : parts + 4]
    up_ref = refs[parts + 4]
    outs = refs[parts + 5 :]

    @pl.when(place[1] == place[2])
    def _():
        count = before[0].shape[0]
        for old, new in zip(before, outs):
            new[0:count, :] = old[...]
        forward_rows(sources, slots, count, up_ref, width, outs, lambda index: None)


def third_kernel(slots, width, parts, place, *refs):
    sources = refs[:parts]
    before = refs[parts : parts + 4]
    up_ref = refs[parts + 4]
    outs = refs[parts + 5 :]

    @pl.when(place[1] == place[2])
    def _():
        for old, new in zip(before, outs):
            new[...] = old[...]

    @pl.when(place[1] != place[2])
    def _():
        forward_rows(sources, slots, 0, up_ref, width, outs, lambda index: None)


def back_kernel(shards, slices, slots, width, base, stage, keep, has_prev, place, after, *refs):
    refs = list(refs)
    take = lambda n: [refs.pop(0) for _ in range(n)]
    own_in = take(2 if has_prev else 1)
    gather_ref = take(1)[0]
    recv_in = take(shards - 1)
    prev_ref = take(1)[0] if has_prev else None
    up_ref, down_ref, act_ref, slope_ref, side_ref, router_ref = take(6)
    rows_ref, gain_ref = take(2) if keep else (None, None)
    own_out = None if keep else take(1)[0]
    cot_ref = take(1)[0]
    q_ref, acc_ref = take(2) if keep else (None, None)
    parts = [] if keep else take(shards)
    if not keep:
        q_ref = refs[0]
    own = own_in[0][...]
    if has_prev:
        own = (own.astype(F32) + own_in[1][...].astype(F32)).astype(BF16)
    if not keep:
        own_out[...] = own
    cot_ref[0:slots, :] = dot(gather_ref[0], own, (1, 0)).astype(BF16)
    for index in range(1, shards):
        rows = slice(index * slots, (index + 1) * slots)
        value = recv_in[index - 1][base : base + slots, :]
        if has_prev:
            value = (value.astype(F32) + prev_ref[rows, :].astype(F32)).astype(BF16)
        cot_ref[rows, :] = value

    @pl.when(place[1] + stage >= place[2])
    def _():
        hidden, feat = down_ref.shape
        lanes = 128
        every = cot_ref.shape[0]

        def block(index, comb):
            span = pl.ds(pl.multiple_of(index * width, width), width)
            t = dot(cot_ref[...], down_ref[span, :], (1, 1))
            prod = act_ref[:, span].astype(F32) * t
            for start in range(0, width, lanes):
                comb = comb + prod[:, start : start + lanes]
            q_ref[:, span] = (slope_ref[:, span].astype(F32) * t).astype(BF16)
            return comb

        comb = lax.fori_loop(0, hidden // width, block, jnp.zeros((every, lanes), F32))
        comb_c = jnp.sum(comb, axis=-1, keepdims=True)
        experts = router_ref.shape[0]
        ids = iota((every, experts), 1)
        pull = jnp.where(ids == place[0] // slices, comb_c * side_ref[:, 1:2], 0.0)
        pull = pull + jnp.where(ids.astype(F32) == side_ref[:, 3:4], comb_c * side_ref[:, 2:3], 0.0)
        if keep:
            acc_ref[...] = jnp.zeros_like(acc_ref)
            rest, routed = pull, jnp.zeros((experts, feat), F32)
            for _ in range(3):
                piece = rest.astype(BF16)
                rest = rest - piece.astype(F32)
                routed = routed + dot(piece, rows_ref[...], (0, 0))
            acc_ref[0:experts, :] = routed
        wide = min(FEAT_WIDTH, feat)
        for start in range(0, feat, wide):
            cols = slice(start, start + wide)
            term = dot(q_ref[...], up_ref[cols, :], (1, 1))
            for expert in range(experts):
                term = term + pull[:, expert : expert + 1] * router_ref[expert : expert + 1, cols]
            if keep:
                gained = jnp.sum(term * rows_ref[:, cols].astype(F32), axis=0, keepdims=True)
                acc_ref[experts : experts + 1, cols] = gained / gain_ref[:, cols]
            for index, part in enumerate(parts):
                part[:, cols] = term[index * slots : (index + 1) * slots, :].astype(BF16)


def owner_kernel(shards, stage, place, *refs):
    parts = refs[:shards]
    own_ref, x_ref, gain_ref, scatter_ref, gather_ref = refs[shards : shards + 5]
    own_out, sends = refs[shards + 5], refs[shards + 6 :]

    @pl.when(place[1] == place[2] - stage)
    def _():
        gh = dot(scatter_ref[0], parts[0][...], (1, 0))
        for step in range(1, shards):
            gh = gh + dot(scatter_ref[step], parts[step][...], (1, 0))
        x = x_ref[...].astype(F32)
        inverse = row_norm(x)
        normed = x * inverse
        scaled = gh * gain_ref[...]
        center = jnp.mean(scaled * normed, axis=-1, keepdims=True)
        gx = (own_ref[...].astype(F32) + inverse * (scaled - normed * center)).astype(BF16)
        own_out[...] = gx
        for step in range(1, shards):
            sends[step - 1][...] = dot(gather_ref[step], gx, (1, 0)).astype(BF16)


def weight_kernel(rows_ref, q_ref, cot_ref, side_ref, act_ref, up_ref, down_ref, turned, y_ref):
    @pl.when(pl.program_id(0) == 0)
    def _():
        turned[...] = rows_ref[...].astype(F32).T.astype(BF16)
        y_ref[...] = (side_ref[:, 0:1] * cot_ref[...].astype(F32)).astype(BF16)

    up_ref[...] = dot(turned[...], q_ref[...], (1, 0)).astype(BF16)
    down_ref[...] = dot(act_ref[...], y_ref[...], (0, 0)).astype(BF16)


def finish_kernel(shards, experts, *refs):
    total = refs[0][...]
    for ref in refs[1:shards]:
        total = total + ref[...]
    refs[shards][...] = total[0:experts, :]
    refs[shards + 1][...] = total[experts : experts + 1, :]


def body(
    layer_inputs, out_cotangent, expert_routes, norm_gain, router_weight, up_weight, down_weight
):
    sections = lax.axis_size("section")
    section_id = lax.axis_index("section")
    shards = lax.axis_size("expert")
    shard_id = lax.axis_index("expert")
    micro, rows, feat = layer_inputs.shape[1:]
    router = router_weight[0]
    experts = router.shape[0]
    up = up_weight[0]
    down = down_weight[0]
    hidden = up.shape[1]
    slices = shards // experts
    total = micro * rows
    cap = rows // BLOCK_ROWS * BLOCK_CAP if rows % BLOCK_ROWS == 0 else rows
    slots = micro * cap
    sent = slots + AUX
    last = sections - 1
    x = layer_inputs[0].reshape(total, feat)
    cot = out_cotangent.reshape(total, feat)
    chosen = lax.dynamic_slice_in_dim(expert_routes[0], shard_id * rows, rows, 1).reshape(total, 2)
    gain = norm_gain
    place = jnp.stack([shard_id, section_id, jnp.int32(last)]).astype(jnp.int32)
    steps = list(range(shards))
    split = max(1, shards // 2)
    width = min(1024, hidden)
    blocks = hidden // width

    def sds(shape, dtype=BF16):
        return jax.ShapeDtypeStruct(shape, dtype)

    def move(value, pairs):
        flat = [(sz * sections + ss, dz * sections + ds) for (ss, sz), (ds, dz) in pairs]
        return lax.ppermute(value, ("expert", "section"), flat)

    def spread(value, step, sources, drop):
        return move(
            value,
            [((s, z), (s - drop, (z + step) % shards)) for s in sources for z in range(shards) if s - drop >= 0],
        )

    def any_place():
        return pl.BlockSpec(memory_space=pl.ANY)

    everyone = list(range(sections))
    far = [pltpu.with_memory_space_constraint(array, pltpu.HBM) for array in (x, cot, gain, router, up, down)]
    hbm = pl.BlockSpec(memory_space=pltpu.HBM)
    prep = pl.pallas_call(
        functools.partial(prep_kernel, shards, slices, rows, slots, cap),
        out_shape=[sds((sent, feat))] * shards
        + [sds((sent + slots, feat))] * (shards - 1)
        + [sds((shards, slots, total)), sds((shards, total, slots)), sds((total, feat))],
        in_specs=[smem()] + [hbm] * 4 + [vmem()] * 2,
        out_specs=[vmem()] * (2 * shards + 2),
        scratch_shapes=[pltpu.VMEM((total, feat), BF16)] * 2
        + [pltpu.VMEM(gain.shape, F32), pltpu.VMEM(router.shape, F32), pltpu.SemaphoreType.DMA((4,))],
        compiler_params=params(),
        cost_estimate=cost(1e7, 4e6),
        name="prep",
    )(place, *far[:4], chosen, chosen.T)
    h_send, c_send = prep[:shards], [None] + list(prep[shards : 2 * shards - 1])
    gather, scatter, own = prep[2 * shards - 1 :]
    first_recv = [None] + [spread(c_send[step], step, [last], 0) for step in steps[1:]]
    gather_next = move(gather, [((s - 1, z), (s, z)) for s in everyone[1:] for z in range(shards)])
    every = shards * slots
    half = split * slots

    def forward(kernel, sources, extra, extra_specs, count, more, scratch):
        return list(
            pl.pallas_call(
                functools.partial(kernel, slots, width, len(sources)),
                out_shape=[sds((count, hidden))] * 2 + [sds((count, feat)), sds((count, SIDES), F32)] + more,
                in_specs=[smem()] + [vmem()] * len(sources) + extra_specs,
                out_specs=[vmem()] * (4 + len(more)),
                scratch_shapes=scratch,
                compiler_params=params(),
                cost_estimate=cost(2 * half * feat * hidden, 2 * feat * hidden),
            )(place, *sources, *extra)
        )

    outs = forward(
        first_kernel, [h_send[0]] + first_recv[1:split], far[4:], [hbm] * 2, half,
        [pltpu.VMEM(up.shape, BF16), pltpu.VMEM(down.shape, BF16)], [pltpu.SemaphoreType.DMA((blocks + 1,))],
    )
    near = [pltpu.with_memory_space_constraint(array, pltpu.VMEM) for array in outs[4:]]
    kept = outs[:4]
    flag_value = kept[3]
    if shards > split:
        extra = [gather_next] + kept + near[:1]
        kept = forward(second_kernel, first_recv[split:], extra, [any_place()] + [vmem()] * 5, every, [], [])

    def back(after, stage, recv, base, own_recv, own, prev):
        has_prev = prev is not None
        keep = stage == last
        args = [place, after] + ([own_recv, own] if has_prev else [own]) + [gather]
        args += [recv[step] for step in steps[1:]]
        args += [prev] * int(has_prev) + near + [kept[0], kept[1], kept[3], router]
        args += [kept[2], gain] * int(keep)
        outs = pl.pallas_call(
            functools.partial(back_kernel, shards, slices, slots, min(2 * width, hidden), base, stage, keep, has_prev),
            out_shape=([] if keep else [sds((total, feat))])
            + [sds((every, feat))]
            + ([sds((every, hidden)), sds((-(-(experts + 1) // 8) * 8, feat), F32)] if keep else [sds((slots, feat))] * shards),
            in_specs=[smem(), any_place()] + [vmem()] * (len(args) - 2),
            out_specs=[vmem()] * (3 if keep else 2 + shards),
            scratch_shapes=[] if keep else [pltpu.VMEM((every, hidden), BF16)],
            compiler_params=params(12 + every * feat * 8 // (1024 * 1024)),
            cost_estimate=cost(4 * every * feat * hidden, 4 * feat * hidden),
            name="back",
        )(*args)
        return list(outs)

    flag = move(flag_value, [((s, z), (s - 1, z)) for s in [last] for z in range(shards)])
    recv, base, own_recv, prev = first_recv, sent, None, None
    for stage in range(last):
        own, prev, *parts = back(flag, stage, recv, base, own_recv, own, prev)
        section = last - stage
        partial = [parts[0]]
        for step in steps[1:]:
            partial.append(spread(parts[step], -step, [section], 0))
        if stage == 0:
            later = lax.optimization_barrier((flag, *h_send[1:]))[1:]
            h_recv = [spread(value, step, everyone[:-1], 0) for step, value in zip(steps[1:], later)]
            kept = forward(third_kernel, [h_send[0]] + h_recv, kept + near[:1], [vmem()] * 5, every, [], [])
        outs = pl.pallas_call(
            functools.partial(owner_kernel, shards, stage),
            out_shape=[sds((total, feat))] + [sds((slots, feat))] * (shards - 1),
            in_specs=[smem()] + [vmem()] * (shards + 5),
            out_specs=[vmem()] * shards,
            compiler_params=params(),
            cost_estimate=cost(1e7, 4e6),
            name="owner",
        )(place, *partial, own, x, gain, scatter, gather_next)
        recv = [None]
        for step in steps[1:]:
            recv.append(spread(outs[step], step, [section], 1))
        own_recv = spread(outs[0], 0, [section], 1)
        base = 0
    cots, q, acc = back(flag, last, recv, base, own_recv, own, prev)
    sums = [acc] + [spread(acc, step, everyone, 0) for step in steps[1:]]
    whole = lambda array: pl.BlockSpec(array.shape, lambda i: (0,) * array.ndim)
    cut = min(GRAD_WIDTH, hidden)
    column = pl.BlockSpec((every, cut), lambda i: (0, i))
    up_grad, down_grad = pl.pallas_call(
        weight_kernel,
        grid=(hidden // cut,),
        out_shape=[sds((feat, hidden)), sds((hidden, feat))],
        in_specs=[whole(kept[2]), column, whole(cots), whole(kept[3]), column],
        out_specs=[pl.BlockSpec((feat, cut), lambda i: (0, i)), pl.BlockSpec((cut, feat), lambda i: (i, 0))],
        scratch_shapes=[pltpu.VMEM((feat, every), BF16), pltpu.VMEM((every, feat), BF16)],
        compiler_params=params(30),
        cost_estimate=cost(4 * every * feat * hidden, 4 * feat * hidden),
        name="weights",
    )(kept[2], q, cots, kept[3], kept[0])
    router_grad, gain_grad = pl.pallas_call(
        functools.partial(finish_kernel, shards, experts),
        out_shape=[sds((experts, feat), F32), sds((1, feat), F32)],
        in_specs=[vmem()] * shards,
        out_specs=[vmem()] * 2,
        compiler_params=params(),
        name="finish",
    )(*sums)
    return (up_grad[None], down_grad[None], router_grad[None], gain_grad)


def solution(mesh):
    in_specs = (
        P("section", None, ("groups", "expert"), None),
        P(None, ("groups", "expert"), None),
        P("section", None, "groups", None),
        P("section", None),
        P("section", None, None),
        P("section", None, "expert"),
        P("section", "expert", None),
    )
    out_specs = (
        P("section", "groups", "expert"),
        P("section", "expert", "groups"),
        P("section", "groups", None),
        P("section", "groups"),
    )
    return jax.shard_map(body, mesh=mesh, in_specs=in_specs, out_specs=out_specs, check_vma=False)
```

```python
import functools

import jax
import jax.numpy as jnp
from jax import lax
from jax.experimental import pallas as pl
from jax.experimental.pallas import tpu as pltpu
from jax.sharding import PartitionSpec as P


norm_eps = 1e-06
gelu_coef = 0.7978845608028654
cubic_coef = 0.044715
BLOCK_ROWS = 64
BLOCK_CAP = 40
F32 = jnp.float32
BF16 = jnp.bfloat16
AUX = 8
SIDES = 4
FEAT_WIDTH = 256
GRAD_WIDTH = 1024


def vmem():
    return pl.BlockSpec(memory_space=pltpu.VMEM)


def smem():
    return pl.BlockSpec(memory_space=pltpu.SMEM)


def params(mebi=12):
    return pltpu.CompilerParams(vmem_limit_bytes=mebi * 1024 * 1024)


def cost(flops, nbytes):
    return pl.CostEstimate(flops=int(flops), bytes_accessed=int(nbytes), transcendentals=0)


def dot(a, b, dims):
    return lax.dot_general(a, b, ((dims[0:1], dims[1:2]), ((), ())), preferred_element_type=F32)


def iota(shape, dim):
    return lax.broadcasted_iota(jnp.int32, shape, dim)


def row_norm(values):
    mean_sq = jnp.mean(values * values, axis=-1, keepdims=True)
    return lax.rsqrt(mean_sq + norm_eps)


def eye(size):
    return (iota((size, size), 0) == iota((size, size), 1)).astype(F32)


def prep_kernel(
    shards, slices, rows, slots, cap, place, x_far, cot_far, gain_far, router_far, col_ref, row_ref, *outs
):
    x_ref, cot_ref, gain_ref, router_ref, sems = outs[-5:]
    outs = outs[:-5]
    loads = [
        pltpu.make_async_copy(source, target, sems.at[index])
        for index, (source, target) in enumerate([(x_far, x_ref), (cot_far, cot_ref), (gain_far, gain_ref), (router_far, router_ref)])
    ]
    for load in loads:
        load.start()
    for load in loads:
        load.wait()
    h_outs, c_outs = outs[:shards], outs[shards : 2 * shards - 1]
    gather_ref, scatter_ref, own_ref = outs[2 * shards - 1 :]
    me = place[0]
    is_last = place[1] == place[2]
    total = x_ref.shape[0]
    experts = router_ref.shape[0]
    x = x_ref[...].astype(F32)
    h32 = (x * row_norm(x)) * gain_ref[...]
    h = h32.astype(BF16)
    logits = lax.dot_general(
        h.astype(F32), router_ref[...], (((1,), (1,)), ((), ())),
        preferred_element_type=F32, precision=lax.Precision.HIGHEST,
    )
    scores = 1.0 / (1.0 + jnp.exp(-logits))
    ids = iota((total, experts), 1)
    hits = jnp.logical_or(col_ref[:, 0:1] == ids, col_ref[:, 1:2] == ids).astype(F32)
    totals = jnp.sum(scores * hits, axis=-1, keepdims=True)
    weights = scores * hits / totals
    slopes = scores * (1.0 - scores) / totals
    first, second = iota((total, total), 0), iota((total, total), 1)
    same = (first // rows) == (second // rows)
    before = jnp.logical_and(same, second < first).astype(BF16)
    after = jnp.logical_and(same, first < second).astype(BF16)
    base_col = (iota((total, experts), 0) // rows * cap).astype(F32)
    slot_col = jnp.where(hits > 0.0, dot(before, hits.astype(BF16), (1, 0)) + base_col, -1.0)
    ids_row = iota((experts, total), 0)
    hits_row = jnp.logical_or(row_ref[0:1, :] == ids_row, row_ref[1:2, :] == ids_row).astype(F32)
    base_row = (iota((experts, total), 1) // rows * cap).astype(F32)
    slot_row = jnp.where(hits_row > 0.0, dot(hits_row.astype(BF16), after, (1, 0)) + base_row, -1.0)
    cot = cot_ref[...]
    own_ref[...] = jnp.where(is_last, cot.astype(F32), 0.0).astype(BF16)
    slot_lane = iota((total, slots), 1).astype(F32)
    slot_sub = iota((slots, total), 0).astype(F32)
    for step in range(shards):
        expert = lax.rem(me + step, shards) // slices
        mine = (ids == expert).astype(F32)
        slot_c = jnp.sum(slot_col * mine, axis=-1, keepdims=True)
        slot_r = jnp.sum(slot_row * (ids_row == expert).astype(F32), axis=0, keepdims=True)
        scatter = (slot_c == slot_lane).astype(F32)
        gather = (slot_r == slot_sub).astype(F32).astype(BF16)
        weight_c = jnp.sum(weights * mine, axis=-1, keepdims=True)
        rest = hits * (1.0 - mine)
        slope_c = jnp.sum(slopes * mine, axis=-1, keepdims=True)
        slope_o = jnp.sum(slopes * rest, axis=-1, keepdims=True)
        other_c = jnp.sum(ids.astype(F32) * rest, axis=-1, keepdims=True)
        sides = [weight_c, (1.0 - weight_c) * slope_c, 0.0 - weight_c * slope_o, other_c]
        aux = jnp.zeros((AUX, slots), F32)
        aux_id = iota((AUX, slots), 0)
        for index, side in enumerate(sides):
            side_r = jnp.sum(scatter * side, axis=0, keepdims=True)
            high = side_r.astype(BF16).astype(F32)
            aux = jnp.where(aux_id == 2 * index, high, jnp.where(aux_id == 2 * index + 1, side_r - high, aux))
        aux = aux.astype(BF16)
        picked = dot(gather, h, (1, 0)).astype(BF16)
        for target in [h_outs[step]] + ([c_outs[step - 1]] if step else []):
            target[0:slots, :] = picked
            target[slots : slots + AUX, :] = jnp.zeros((AUX, x.shape[1]), BF16)
            target[slots : slots + AUX, 0:slots] = aux
        if step:
            c_outs[step - 1][slots + AUX :, :] = dot(gather, cot, (1, 0)).astype(BF16)
        gather_ref[step] = gather
        scatter_ref[step] = scatter.astype(BF16)


def forward_rows(sources, slots, row0, up_ref, width, outs, ready):
    act_ref, slope_ref, rows_ref, side_ref = outs
    count = len(sources) * slots
    for index, source in enumerate(sources):
        span = slice(row0 + index * slots, row0 + (index + 1) * slots)
        value = source[0 : slots + AUX, :].astype(F32)
        rows_ref[span, :] = value[0:slots, :].astype(BF16)
        for column in range(SIDES):
            low = slots + 2 * column
            side_r = value[low : low + 1, 0:slots] + value[low + 1 : low + 2, 0:slots]
            side_ref[span, column : column + 1] = jnp.sum(eye(slots) * side_r, axis=-1, keepdims=True)
    rows = slice(row0, row0 + count)

    def block(index, carry):
        ready(index)
        span = pl.ds(pl.multiple_of(index * width, width), width)
        u = dot(rows_ref[rows, :], up_ref[:, span], (1, 0))
        square = u * u
        tanh_val = jnp.tanh(gelu_coef * (u + cubic_coef * square * u))
        half = 0.5 * (1.0 + tanh_val)
        act_ref[rows, span] = (u * half).astype(BF16)
        slope = half + 0.5 * u * (1.0 - tanh_val * tanh_val) * (gelu_coef * (1.0 + 3.0 * cubic_coef * square))
        slope_ref[rows, span] = (slope * side_ref[rows, 0:1]).astype(BF16)
        return carry

    lax.fori_loop(0, up_ref.shape[1] // width, block, 0)


def first_kernel(slots, width, parts, place, *refs):
    sources = refs[:parts]
    up_far, down_far = refs[parts : parts + 2]
    outs = refs[parts + 2 : parts + 6]
    up_ref, down_ref, sems = refs[parts + 6 :]
    blocks = up_ref.shape[1] // width
    last = place[1] == place[2]

    def column_load(index):
        span = pl.ds(pl.multiple_of(index * width, width), width)
        return pltpu.make_async_copy(up_far.at[:, span], up_ref.at[:, span], sems.at[index])

    down_load = pltpu.make_async_copy(down_far, down_ref, sems.at[blocks])
    for index in range(blocks):
        column_load(index).start()
    down_load.start()

    @pl.when(last)
    def _():
        forward_rows(sources, slots, 0, up_ref, width, outs, lambda index: column_load(index).wait())

    @pl.when(jnp.logical_not(last))
    def _():
        for index in range(blocks):
            column_load(index).wait()

    down_load.wait()


def second_kernel(slots, width, parts, place, *refs):
    sources = refs[:parts]
    refs = refs[:parts] + refs[parts + 1 :]
    before = refs[parts : parts + 4]
    up_ref = refs[parts + 4]
    outs = refs[parts + 5 :]

    @pl.when(place[1] == place[2])
    def _():
        count = before[0].shape[0]
        for old, new in zip(before, outs):
            new[0:count, :] = old[...]
        forward_rows(sources, slots, count, up_ref, width, outs, lambda index: None)


def third_kernel(slots, width, parts, place, *refs):
    sources = refs[:parts]
    before = refs[parts : parts + 4]
    up_ref = refs[parts + 4]
    outs = refs[parts + 5 :]

    @pl.when(place[1] == place[2])
    def _():
        for old, new in zip(before, outs):
            new[...] = old[...]

    @pl.when(place[1] != place[2])
    def _():
        forward_rows(sources, slots, 0, up_ref, width, outs, lambda index: None)


def back_kernel(shards, slices, slots, width, base, stage, keep, has_prev, place, after, *refs):
    refs = list(refs)
    take = lambda n: [refs.pop(0) for _ in range(n)]
    own_in = take(2 if has_prev else 1)
    gather_ref = take(1)[0]
    recv_in = take(shards - 1)
    prev_ref = take(1)[0] if has_prev else None
    up_ref, down_ref, act_ref, slope_ref, side_ref, router_ref = take(6)
    rows_ref, gain_ref = take(2) if keep else (None, None)
    own_out = None if keep else take(1)[0]
    cot_ref = take(1)[0]
    q_ref, acc_ref = take(2) if keep else (None, None)
    parts = [] if keep else take(shards)
    if not keep:
        q_ref = refs[0]
    own = own_in[0][...]
    if has_prev:
        own = (own.astype(F32) + own_in[1][...].astype(F32)).astype(BF16)
    if not keep:
        own_out[...] = own
    cot_ref[0:slots, :] = dot(gather_ref[0], own, (1, 0)).astype(BF16)
    for index in range(1, shards):
        rows = slice(index * slots, (index + 1) * slots)
        value = recv_in[index - 1][base : base + slots, :]
        if has_prev:
            value = (value.astype(F32) + prev_ref[rows, :].astype(F32)).astype(BF16)
        cot_ref[rows, :] = value

    @pl.when(place[1] + stage >= place[2])
    def _():
        hidden, feat = down_ref.shape
        lanes = 128
        every = cot_ref.shape[0]

        def block(index, comb):
            span = pl.ds(pl.multiple_of(index * width, width), width)
            t = dot(cot_ref[...], down_ref[span, :], (1, 1))
            prod = act_ref[:, span].astype(F32) * t
            for start in range(0, width, lanes):
                comb = comb + prod[:, start : start + lanes]
            q_ref[:, span] = (slope_ref[:, span].astype(F32) * t).astype(BF16)
            return comb

        comb = lax.fori_loop(0, hidden // width, block, jnp.zeros((every, lanes), F32))
        comb_c = jnp.sum(comb, axis=-1, keepdims=True)
        experts = router_ref.shape[0]
        ids = iota((every, experts), 1)
        pull = jnp.where(ids == place[0] // slices, comb_c * side_ref[:, 1:2], 0.0)
        pull = pull + jnp.where(ids.astype(F32) == side_ref[:, 3:4], comb_c * side_ref[:, 2:3], 0.0)
        if keep:
            acc_ref[...] = jnp.zeros_like(acc_ref)
            rest, routed = pull, jnp.zeros((experts, feat), F32)
            for _ in range(3):
                piece = rest.astype(BF16)
                rest = rest - piece.astype(F32)
                routed = routed + dot(piece, rows_ref[...], (0, 0))
            acc_ref[0:experts, :] = routed
        wide = min(FEAT_WIDTH, feat)
        for start in range(0, feat, wide):
            cols = slice(start, start + wide)
            term = dot(q_ref[...], up_ref[cols, :], (1, 1))
            for expert in range(experts):
                term = term + pull[:, expert : expert + 1] * router_ref[expert : expert + 1, cols]
            if keep:
                gained = jnp.sum(term * rows_ref[:, cols].astype(F32), axis=0, keepdims=True)
                acc_ref[experts : experts + 1, cols] = gained / gain_ref[:, cols]
            for index, part in enumerate(parts):
                part[:, cols] = term[index * slots : (index + 1) * slots, :].astype(BF16)


def owner_kernel(shards, stage, place, *refs):
    parts = refs[:shards]
    own_ref, x_ref, gain_ref, scatter_ref, gather_ref = refs[shards : shards + 5]
    own_out, sends = refs[shards + 5], refs[shards + 6 :]

    @pl.when(place[1] == place[2] - stage)
    def _():
        gh = dot(scatter_ref[0], parts[0][...], (1, 0))
        for step in range(1, shards):
            gh = gh + dot(scatter_ref[step], parts[step][...], (1, 0))
        x = x_ref[...].astype(F32)
        inverse = row_norm(x)
        normed = x * inverse
        scaled = gh * gain_ref[...]
        center = jnp.mean(scaled * normed, axis=-1, keepdims=True)
        gx = (own_ref[...].astype(F32) + inverse * (scaled - normed * center)).astype(BF16)
        own_out[...] = gx
        for step in range(1, shards):
            sends[step - 1][...] = dot(gather_ref[step], gx, (1, 0)).astype(BF16)


def weight_kernel(rows_ref, q_ref, cot_ref, side_ref, act_ref, up_ref, down_ref, turned, y_ref):
    @pl.when(pl.program_id(0) == 0)
    def _():
        turned[...] = rows_ref[...].astype(F32).T.astype(BF16)
        y_ref[...] = (side_ref[:, 0:1] * cot_ref[...].astype(F32)).astype(BF16)

    up_ref[...] = dot(turned[...], q_ref[...], (1, 0)).astype(BF16)
    down_ref[...] = dot(act_ref[...], y_ref[...], (0, 0)).astype(BF16)


def finish_kernel(shards, experts, *refs):
    total = refs[0][...]
    for ref in refs[1:shards]:
        total = total + ref[...]
    refs[shards][...] = total[0:experts, :]
    refs[shards + 1][...] = total[experts : experts + 1, :]


def body(
    layer_inputs, out_cotangent, expert_routes, norm_gain, router_weight, up_weight, down_weight
):
    sections = lax.axis_size("section")
    section_id = lax.axis_index("section")
    shards = lax.axis_size("expert")
    shard_id = lax.axis_index("expert")
    micro, rows, feat = layer_inputs.shape[1:]
    router = router_weight[0]
    experts = router.shape[0]
    up = up_weight[0]
    down = down_weight[0]
    hidden = up.shape[1]
    slices = shards // experts
    total = micro * rows
    cap = rows // BLOCK_ROWS * BLOCK_CAP if rows % BLOCK_ROWS == 0 else rows
    slots = micro * cap
    sent = slots + AUX
    last = sections - 1
    x = layer_inputs[0].reshape(total, feat)
    cot = out_cotangent.reshape(total, feat)
    chosen = lax.dynamic_slice_in_dim(expert_routes[0], shard_id * rows, rows, 1).reshape(total, 2)
    gain = norm_gain
    place = jnp.stack([shard_id, section_id, jnp.int32(last)]).astype(jnp.int32)
    steps = list(range(shards))
    split = max(1, shards // 2)
    width = min(1024, hidden)
    blocks = hidden // width

    def sds(shape, dtype=BF16):
        return jax.ShapeDtypeStruct(shape, dtype)

    def move(value, pairs):
        flat = [(sz * sections + ss, dz * sections + ds) for (ss, sz), (ds, dz) in pairs]
        return lax.ppermute(value, ("expert", "section"), flat)

    def spread(value, step, sources, drop):
        return move(
            value,
            [((s, z), (s - drop, (z + step) % shards)) for s in sources for z in range(shards) if s - drop >= 0],
        )

    def any_place():
        return pl.BlockSpec(memory_space=pl.ANY)

    everyone = list(range(sections))
    far = [pltpu.with_memory_space_constraint(array, pltpu.HBM) for array in (x, cot, gain, router, up, down)]
    hbm = pl.BlockSpec(memory_space=pltpu.HBM)
    prep = pl.pallas_call(
        functools.partial(prep_kernel, shards, slices, rows, slots, cap),
        out_shape=[sds((sent, feat))] * shards
        + [sds((sent + slots, feat))] * (shards - 1)
        + [sds((shards, slots, total)), sds((shards, total, slots)), sds((total, feat))],
        in_specs=[smem()] + [hbm] * 4 + [vmem()] * 2,
        out_specs=[vmem()] * (2 * shards + 2),
        scratch_shapes=[pltpu.VMEM((total, feat), BF16)] * 2
        + [pltpu.VMEM(gain.shape, F32), pltpu.VMEM(router.shape, F32), pltpu.SemaphoreType.DMA((4,))],
        compiler_params=params(),
        cost_estimate=cost(1e7, 4e6),
        name="prep",
    )(place, *far[:4], chosen, chosen.T)
    h_send, c_send = prep[:shards], [None] + list(prep[shards : 2 * shards - 1])
    gather, scatter, own = prep[2 * shards - 1 :]
    first_recv = [None]
    for step in steps[1:]:
        first_recv.append(spread(c_send[step], step, [last], 0))
    every = shards * slots
    half = split * slots

    def forward(kernel, sources, extra, extra_specs, count, more, scratch):
        return list(
            pl.pallas_call(
                functools.partial(kernel, slots, width, len(sources)),
                out_shape=[sds((count, hidden))] * 2 + [sds((count, feat)), sds((count, SIDES), F32)] + more,
                in_specs=[smem()] + [vmem()] * len(sources) + extra_specs,
                out_specs=[vmem()] * (4 + len(more)),
                scratch_shapes=scratch,
                compiler_params=params(),
                cost_estimate=cost(2 * half * feat * hidden, 2 * feat * hidden),
            )(place, *sources, *extra)
        )

    outs = forward(
        first_kernel, [h_send[0]] + first_recv[1:split], far[4:], [hbm] * 2, half,
        [pltpu.VMEM(up.shape, BF16), pltpu.VMEM(down.shape, BF16)], [pltpu.SemaphoreType.DMA((blocks + 1,))],
    )
    near = [pltpu.with_memory_space_constraint(array, pltpu.VMEM) for array in outs[4:]]
    kept = outs[:4]
    flag_value = kept[3]
    gather_late = lax.optimization_barrier((gather, kept[3]))[0]
    gather_next = move(gather_late, [((s - 1, z), (s, z)) for s in everyone[1:] for z in range(shards)])
    if shards > split:
        extra = [gather_next] + kept + near[:1]
        kept = forward(second_kernel, first_recv[split:], extra, [any_place()] + [vmem()] * 5, every, [], [])

    def back(after, stage, recv, base, own_recv, own, prev):
        has_prev = prev is not None
        keep = stage == last
        args = [place, after] + ([own_recv, own] if has_prev else [own]) + [gather]
        args += [recv[step] for step in steps[1:]]
        args += [prev] * int(has_prev) + near + [kept[0], kept[1], kept[3], router]
        args += [kept[2], gain] * int(keep)
        outs = pl.pallas_call(
            functools.partial(back_kernel, shards, slices, slots, min(2 * width, hidden), base, stage, keep, has_prev),
            out_shape=([] if keep else [sds((total, feat))])
            + [sds((every, feat))]
            + ([sds((every, hidden)), sds((-(-(experts + 1) // 8) * 8, feat), F32)] if keep else [sds((slots, feat))] * shards),
            in_specs=[smem(), any_place()] + [vmem()] * (len(args) - 2),
            out_specs=[vmem()] * (3 if keep else 2 + shards),
            scratch_shapes=[] if keep else [pltpu.VMEM((every, hidden), BF16)],
            compiler_params=params(12 + every * feat * 8 // (1024 * 1024)),
            cost_estimate=cost(4 * every * feat * hidden, 4 * feat * hidden),
            name="back",
        )(*args)
        return list(outs)

    flag = move(flag_value, [((s, z), (s - 1, z)) for s in [last] for z in range(shards)])
    recv, base, own_recv, prev = first_recv, sent, None, None
    for stage in range(last):
        own, prev, *parts = back(flag, stage, recv, base, own_recv, own, prev)
        section = last - stage
        partial = [parts[0]]
        for step in steps[1:]:
            partial.append(spread(parts[step], -step, [section], 0))
        if stage == 0:
            later = lax.optimization_barrier((flag, *h_send[1:]))[1:]
            h_recv = []
            for step, value in zip(steps[1:], later):
                h_recv.append(spread(value, step, everyone[:-1], 0))
            kept = forward(third_kernel, [h_send[0]] + h_recv, kept + near[:1], [vmem()] * 5, every, [], [])
        outs = pl.pallas_call(
            functools.partial(owner_kernel, shards, stage),
            out_shape=[sds((total, feat))] + [sds((slots, feat))] * (shards - 1),
            in_specs=[smem()] + [vmem()] * (shards + 5),
            out_specs=[vmem()] * shards,
            compiler_params=params(),
            cost_estimate=cost(1e7, 4e6),
            name="owner",
        )(place, *partial, own, x, gain, scatter, gather_next)
        recv = [None]
        for step in steps[1:]:
            recv.append(spread(outs[step], step, [section], 1))
        own_recv = spread(outs[0], 0, [section], 1)
        base = 0
    cots, q, acc = back(flag, last, recv, base, own_recv, own, prev)
    sums = [acc] + [spread(acc, step, everyone, 0) for step in steps[1:]]
    whole = lambda array: pl.BlockSpec(array.shape, lambda i: (0,) * array.ndim)
    cut = min(GRAD_WIDTH, hidden)
    column = pl.BlockSpec((every, cut), lambda i: (0, i))
    up_grad, down_grad = pl.pallas_call(
        weight_kernel,
        grid=(hidden // cut,),
        out_shape=[sds((feat, hidden)), sds((hidden, feat))],
        in_specs=[whole(kept[2]), column, whole(cots), whole(kept[3]), column],
        out_specs=[pl.BlockSpec((feat, cut), lambda i: (0, i)), pl.BlockSpec((cut, feat), lambda i: (i, 0))],
        scratch_shapes=[pltpu.VMEM((feat, every), BF16), pltpu.VMEM((every, feat), BF16)],
        compiler_params=params(30),
        cost_estimate=cost(4 * every * feat * hidden, 4 * feat * hidden),
        name="weights",
    )(kept[2], q, cots, kept[3], kept[0])
    router_grad, gain_grad = pl.pallas_call(
        functools.partial(finish_kernel, shards, experts),
        out_shape=[sds((experts, feat), F32), sds((1, feat), F32)],
        in_specs=[vmem()] * shards,
        out_specs=[vmem()] * 2,
        compiler_params=params(),
        name="finish",
    )(*sums)
    return (up_grad[None], down_grad[None], router_grad[None], gain_grad)


def solution(mesh):
    in_specs = (
        P("section", None, ("groups", "expert"), None),
        P(None, ("groups", "expert"), None),
        P("section", None, "groups", None),
        P("section", None),
        P("section", None, None),
        P("section", None, "expert"),
        P("section", "expert", None),
    )
    out_specs = (
        P("section", "groups", "expert"),
        P("section", "expert", "groups"),
        P("section", "groups", None),
        P("section", "groups"),
    )
    return jax.shard_map(body, mesh=mesh, in_specs=in_specs, out_specs=out_specs, check_vma=False)
```
